256 devices in a mesh: ctx: 32 (over x, z), fsdp: 8 (over y, core).
Axes of the slice: x: 4, y: 4, z: 8, core: 2. Of those that a mesh axis runs over, the one named last changes fastest.
Arguments:
- query_in: bfloat16 [16384, 4096], P('ctx', 'fsdp'), may hold values from -6 to 6
- key_in: bfloat16 [16384, 4096], P('ctx', 'fsdp'), may hold values from -6 to 6
- value_in: bfloat16 [16384, 4096], P('ctx', 'fsdp'), may hold values from -6 to 6
- residues: float32 [16, 256], P(None, 'fsdp'), may hold values from -1.5 to 1.5
- decay_rate: float32 [16, 256], P(None, 'fsdp'), may hold values from 1.5258789e-05 to 0.1
- short_filter: float32 [3, 3, 4096], P(None, None, 'fsdp'), may hold values from -3 to 3
- skip_gain: float32 [1, 4096], P(None, 'fsdp'), may hold values from -3 to 3
Outputs:
- mixed_out: bfloat16 [16384, 4096], P('ctx', 'fsdp')
The draws below stay inside these ranges and needn't reach their ends.
All inputs are finite; a program needn't handle non-finite values.
Results may differ from the reference program's by a relative error of at most 0.001.
Values may be sent and summed in bfloat16 or wider, within the bound.
A program may use at most 320 MiB of HBM per device.

```python
import jax
import jax.numpy as jnp
from jax import lax

D = 4096
FILTERS = 256
MODES = 16
SHORT = 3
SPAN = 512
GS = 16
TOTAL = 16384


def draw_decay_rate(key, part):
    first, second = jax.random.split(jax.random.fold_in(key, 17), 2)
    share = 0.5
    slow = jax.random.uniform(first, (MODES, FILTERS), jnp.float32) < share
    ratio = jax.random.uniform(second, (MODES, FILTERS), jnp.float32)
    low_slow = 0.25 / TOTAL
    high_slow = 2.0 / TOTAL
    slow_rate = jnp.exp(jnp.log(low_slow) + ratio * jnp.log(high_slow / low_slow))
    fast_rate = jnp.exp(jnp.log(high_slow) + ratio * jnp.log(0.1 / high_slow))
    return jnp.where(slow, slow_rate, fast_rate).astype(jnp.float32)


def block_levels(rng, dims, shards, smallest, top_value):
    def one(dim, shards_of):
        heights = jax.random.uniform(jax.random.fold_in(jax.random.fold_in(rng, 6), dim), (shards_of,), jnp.float32, smallest / len(shards), top_value / len(shards))
        return jnp.repeat(jnp.exp(heights), dims[dim] // shards_of).reshape((-1,) + (1,) * (len(dims) - dim - 1))

    factor_of = one(*shards[0])
    for cut in shards[1:]:
        factor_of = factor_of * one(*cut)
    return factor_of


def gaussian(own_key, extent, scale, most, shards=(), dtype=jnp.bfloat16):
    result = scale * jax.random.normal(own_key, extent, jnp.float32)
    if shards:
        result = result * block_levels(own_key, extent, shards, -0.22, 0.18)
    return jnp.clip(result, -most, most).astype(dtype)


def setup_inputs(seed: int = 0) -> dict:
    splits = jax.random.split(jax.random.key(seed), 8)
    query_in = gaussian(splits[0], (TOTAL, D), 1.0, 6.0, ((0, 32), (1, 8)))
    key_in = gaussian(splits[1], (TOTAL, D), 1.0, 6.0, ((0, 32), (1, 8)))
    value_in = gaussian(splits[2], (TOTAL, D), 1.0, 6.0, ((0, 32), (1, 8)))
    residues = gaussian(splits[3], (MODES, FILTERS), MODES ** -0.5, 1.5, ((1, 8),), jnp.float32)
    decay_rate = draw_decay_rate(jax.random.fold_in(splits[7], 71), 0)
    short_filter = gaussian(splits[5], (3, SHORT, D), 0.5, 3.0, ((2, 8),), jnp.float32)
    skip_gain = gaussian(splits[6], (1, D), 0.5, 3.0, ((1, 8),), jnp.float32)
    return {"query_in": query_in, "key_in": key_in, "value_in": value_in, "residues": residues, "decay_rate": decay_rate, "short_filter": short_filter, "skip_gain": skip_gain}


def filter_taps(residues, decay_rate, count):
    norm = jnp.sqrt(-jnp.expm1(-2.0 * decay_rate))
    weight = residues * norm
    steps = jnp.arange(count).astype(jnp.float32)
    return lax.optimization_barrier(jnp.sum(weight[:, :, None] * jnp.exp(-decay_rate[:, :, None] * steps), axis=0))

def toeplitz(taps):
    count = taps.shape[1]
    lag = jnp.arange(count)[:, None] - jnp.arange(count)[None, :]
    picked = jnp.take(taps, jnp.clip(lag, 0, count - 1), axis=1)
    return jnp.where(lag >= 0, picked, jnp.zeros_like(picked))

def short_conv(padded, weights, count):
    width = weights.shape[0]
    total = jnp.zeros((count, weights.shape[1]), jnp.float32)
    for shift_at in range(width):
        begin = width - 1 - shift_at
        total = total + weights[shift_at][None, :] * padded[begin:begin + count]
    return total

def reference(query_in, key_in, value_in, residues, decay_rate, short_filter, skip_gain):
    taps = filter_taps(residues, decay_rate, SPAN)
    toe = toeplitz(taps)
    norm = jnp.sqrt(-jnp.expm1(-2.0 * decay_rate))
    weight = residues * norm
    steps = jnp.arange(SPAN).astype(jnp.float32)
    lead = weight[:, :, None] * jnp.exp(-decay_rate[:, :, None] * (steps + 1.0))
    tail = jnp.exp(-decay_rate[:, :, None] * (SPAN - 1.0 - steps))
    power = jnp.exp(-decay_rate * SPAN)
    high = lax.Precision.HIGHEST
    front = jnp.zeros((SHORT - 1, D), jnp.float32)
    q_short = short_conv(jnp.concatenate([front, query_in.astype(jnp.float32)], 0), short_filter[0], TOTAL)
    k_short = short_conv(jnp.concatenate([front, key_in.astype(jnp.float32)], 0), short_filter[1], TOTAL)
    v_short = short_conv(jnp.concatenate([front, value_in.astype(jnp.float32)], 0), short_filter[2], TOTAL)
    gated = k_short * v_short
    blocks = gated.reshape(TOTAL // SPAN, SPAN, FILTERS, GS)

    def step_block(state, block):
        local = jnp.einsum('gts,sgj->tgj', toe, block, precision=high)
        term = jnp.einsum('ngt,ngj->tgj', lead, state, precision=high)
        fresh = jnp.einsum('ngs,sgj->ngj', tail, block, precision=high)
        return (state * power[:, :, None] + fresh, local + term)
    start = jnp.zeros((MODES, FILTERS, GS), jnp.float32)
    _, convs = lax.scan(step_block, start, blocks)
    long_conv = convs.reshape(TOTAL, D)
    return (q_short * (long_conv + skip_gain[0][None, :] * gated)).astype(jnp.bfloat16)
```

```python
import functools

import jax
import jax.numpy as jnp
from jax import lax
from jax.experimental import pallas as pl
from jax.experimental.pallas import tpu as pltpu
from jax.sharding import PartitionSpec as P

MESH = pl.DeviceIdType.MESH
NX, NZ = 4, 8
SEGS = 8
LANES = 128
FRONT = 8


def to_device(src, dst, send, recv, ctx):
    return pltpu.make_async_remote_copy(
        src_ref=src,
        dst_ref=dst,
        send_sem=send,
        recv_sem=recv,
        device_id={"ctx": ctx},
        device_id_type=MESH,
    )


def one_minus_exp(u):
    series = u * (1 - u / 2 * (1 - u / 3 * (1 - u / 4 * (1 - u / 5 * (1 - u / 6 * (1 - u / 7))))))
    return jnp.where(u < 0.3, series, 1 - jnp.exp(-u))


def scan_segments(value, powers, row):
    for power, step in zip(powers, (1, 2, 4)):
        value = value + power * jnp.where(row >= step, pltpu.roll(value, step, 0), 0.0)
    return value


def split(x):
    high = x.astype(jnp.bfloat16)
    return high, (x - high.astype(jnp.float32)).astype(jnp.bfloat16)


def kernel(
    query, key, value, residues, decay_rate, short_filter, skip_gain,
    out,
    raw, wide, params_r, params_d, filt, skip,
    decay, weight, gated, final, base, qs, lead_hi, lead_lo,
    fresh, lines, edge, rim, delta_own, delta, total, totals, own_sum, far_sum,
    in_sem, line_send, line_recv, delta_send, delta_recv, total_send, total_recv, rim_send, rim_recv,
):
    rows, width = query.shape
    modes, groups = residues.shape
    size = width // groups
    steps = rows // SEGS
    tiles = width // LANES
    f32 = jnp.float32

    me = lax.axis_index("ctx")
    x, z = me // NZ, lax.rem(me, NZ)

    def line_peer(k):
        return x * NZ + lax.rem(z + k, NZ)

    barrier = pltpu.get_barrier_semaphore()

    def here(ctx):
        pl.semaphore_signal(barrier, inc=1, device_id={"ctx": ctx}, device_id_type=MESH)

    for k in range(1, NZ):
        here(line_peer(k))
    for k in range(1, NX):
        pl.when(x >= k)(functools.partial(here, me - k * NZ))
    pl.when((z == 0) & (x > 0))(functools.partial(here, me - 1))

    small = [
        pltpu.make_async_copy(a, b, in_sem.at[i])
        for i, (a, b) in enumerate(
            ((residues, params_r), (decay_rate, params_d), (short_filter, filt), (skip_gain, skip))
        )
    ]
    large = [
        pltpu.make_async_copy(a, raw.at[p], in_sem.at[4 + p])
        for p, a in enumerate((query, key, value))
    ]
    for copy in (small[1], small[0], small[2], large[1], large[2], large[0], small[3]):
        copy.start()

    small[0].wait()
    small[1].wait()
    small[2].wait()
    lane = lax.broadcasted_iota(jnp.int32, (groups, width), 1)
    group = lax.broadcasted_iota(jnp.int32, (groups, width), 0)
    pick = (lane // size == group).astype(f32)
    high = lax.Precision.HIGHEST
    rate = jnp.dot(params_d[...], pick, precision=high, preferred_element_type=f32)
    decay[...] = rate
    residue = jnp.dot(params_r[...], pick, precision=high, preferred_element_type=f32)
    weight[...] = residue * jnp.sqrt(one_minus_exp(2.0 * rate))

    row = lax.broadcasted_iota(jnp.int32, (SEGS, LANES), 0)

    def widen(p):
        for t in range(tiles):
            wide[p, t, 0:FRONT] = jnp.zeros((FRONT, LANES), f32)
            wide[p, t, FRONT:] = raw[p, :, t * LANES : (t + 1) * LANES].astype(f32)

    large[1].wait()
    widen(1)
    large[2].wait()
    widen(2)

    def segments(p, offset, tile):
        return wide[p, tile, pl.ds(FRONT + offset, SEGS, stride=steps)]

    def taps_of(p, cols):
        return [jnp.broadcast_to(filt[p, i : i + 1, cols], (SEGS, LANES)) for i in range(3)]

    def short(taps, now, last, older):
        return taps[0] * now + taps[1] * last + taps[2] * older

    for tile in range(tiles):
        cols = slice(tile * LANES, (tile + 1) * LANES)
        ktaps, vtaps = taps_of(1, cols), taps_of(2, cols)
        rates = [
            jnp.broadcast_to(jnp.exp(-decay[n : n + 1, cols]), (SEGS, LANES)) for n in range(modes)
        ]

        def advance(j, carry, tile=tile, cols=cols, ktaps=ktaps, vtaps=vtaps, rates=rates):
            k1, k2, v1, v2, states = carry
            k0, v0 = segments(1, j, tile), segments(2, j, tile)
            g = short(ktaps, k0, k1, k2) * short(vtaps, v0, v1, v2)
            gated[pl.ds(pl.multiple_of(j * SEGS, SEGS), SEGS), cols] = g
            states = tuple(s * a + g for s, a in zip(states, rates))
            return k0, k1, v0, v1, states

        zero = jnp.zeros((SEGS, LANES), f32)
        first = (
            segments(1, -1, tile), segments(1, -2, tile),
            segments(2, -1, tile), segments(2, -2, tile),
            (zero,) * modes,
        )
        states = lax.fori_loop(0, steps, advance, first, unroll=4)[4]
        for n in range(modes):
            final[n, :, cols] = states[n]
            powers = [jnp.exp(-decay[n : n + 1, cols] * (steps * s)) for s in (1, 2, 4)]
            fresh[n : n + 1, cols] = scan_segments(states[n], powers, row)[SEGS - 1 : SEGS]

    large[0].wait()
    for p in range(3):
        edge[2 * p : 2 * p + 2] = raw[p, rows - 8 : rows].astype(f32)[6:8]
    pl.semaphore_wait(
        barrier, NZ - 1 + NX - 1 - x + jnp.where((z == NZ - 1) & (x < NX - 1), 1, 0)
    )
    last = NX * NZ - 1
    rim_copy = to_device(edge, rim, rim_send, rim_recv, me + 1)
    pl.when(me < last)(rim_copy.start)
    line_copies = {
        k: to_device(fresh, lines.at[z], line_send.at[k], line_recv.at[k], line_peer(k))
        for k in range(1, NZ)
    }
    for k in (4, 3, 5, 2, 6, 1, 7):
        line_copies[k].start()
    lines[z] = fresh[...]

    lane = lax.broadcasted_iota(jnp.int32, (modes, width), 1)
    mode = lax.broadcasted_iota(jnp.int32, (modes, width), 0)
    own = lax.rem(lane, modes) == mode
    flat_rate = jnp.sum(jnp.where(own, decay[...], 0.0), axis=0, keepdims=True)
    flat_weight = jnp.sum(jnp.where(own, weight[...], 0.0), axis=0, keepdims=True)
    for tile in range(tiles):
        cols = slice(tile * LANES, (tile + 1) * LANES)
        rate8 = jnp.broadcast_to(flat_rate[:, cols], (16, LANES))
        row16 = lax.broadcasted_iota(jnp.int32, (16, LANES), 0).astype(f32)
        begin = flat_weight[:, cols] * jnp.exp(-rate8 * (row16 + 1.0))
        jump = jnp.exp(-rate8 * 16.0)

        def lead_rows(i, now, cols=cols, jump=jump):
            at = pl.ds(pl.multiple_of(i * 16, 16), 16)
            hi, lo = split(now)
            lead_hi[at, cols] = hi
            lead_lo[at, cols] = lo
            return now * jump

        lax.fori_loop(0, rows // 16, lead_rows, begin, unroll=4)
    widen(0)
    small[3].wait()

    @pl.when(me == 0)
    def _():
        rim[...] = jnp.zeros_like(rim)

    pl.when(me > 0)(rim_copy.wait_recv)
    for tile in range(tiles):
        cols = slice(tile * LANES, (tile + 1) * LANES)
        for p in range(3):
            wide[p, tile, FRONT - 2 : FRONT] = rim[2 * p : 2 * p + 2, cols]

        def head(p, tile=tile, cols=cols):
            front = wide[p, tile, FRONT - 2 : FRONT + 2]
            return sum(filt[p, i : i + 1, cols] * front[2 - i : 4 - i] for i in range(3))

        true_head = head(1) * head(2)
        for i in range(2):
            at = slice(i * SEGS, i * SEGS + 1)
            delta_own[i : i + 1, cols] = true_head[i : i + 1] - gated[at, cols]
            gated[at, cols] = true_head[i : i + 1]
    delta_copies = {
        k: to_device(delta_own, delta.at[z], delta_send.at[k], delta_recv.at[k], line_peer(k))
        for k in range(1, NZ)
    }
    for k in (4, 3, 5, 2, 6, 1, 7):
        delta_copies[k].start()
    delta[z] = delta_own[...]

    for tile in range(tiles):
        cols = slice(tile * LANES, (tile + 1) * LANES)
        qtaps = taps_of(0, cols)
        gain = jnp.broadcast_to(skip[0:1, cols], (SEGS, LANES))
        d0, d1 = delta_own[0:1, cols], delta_own[1:2, cols]
        rates, weights, entering = [], [], []
        for n in range(modes):
            rate = decay[n : n + 1, cols]
            powers = [jnp.exp(-rate * (steps * s)) for s in (1, 2, 4)]
            extra = jnp.exp(-rate * (steps - 1.0)) * d0 + jnp.exp(-rate * (steps - 2.0)) * d1
            state = final[n, :, cols] + jnp.where(row == 0, extra, 0.0)
            state = scan_segments(state, powers, row)
            entering.append(jnp.where(row >= 1, pltpu.roll(state, 1, 0), 0.0))
            rates.append(jnp.broadcast_to(jnp.exp(-rate), (SEGS, LANES)))
            weights.append(jnp.broadcast_to(weight[n : n + 1, cols], (SEGS, LANES)))

        def respond(j, carry, tile=tile, cols=cols, qtaps=qtaps, gain=gain, rates=rates, weights=weights):
            q1, q2, states = carry
            q0 = segments(0, j, tile)
            g = gated[pl.ds(pl.multiple_of(j * SEGS, SEGS), SEGS), cols]
            states = tuple(s * a + g for s, a in zip(states, rates))
            terms = [s * w for s, w in zip(states, weights)] + [gain * g]
            while len(terms) > 1:
                terms = [sum(terms[i : i + 2]) for i in range(0, len(terms), 2)]
            q = short(qtaps, q0, q1, q2)
            at = pl.ds(j, SEGS, stride=steps)
            base[tile, at] = q * terms[0]
            qs[tile, at] = q
            return q0, q1, states

        first = (segments(0, -1, tile), segments(0, -2, tile), tuple(entering))
        lax.fori_loop(0, steps, respond, first, unroll=4)

    block = jnp.exp(-decay[...] * rows)
    late0 = jnp.exp(-decay[...] * (rows - 1.0))
    late1 = jnp.exp(-decay[...] * (rows - 2.0))
    hop = jnp.exp(-decay[...] * (rows * NZ))
    for k in range(1, NZ):
        line_copies[k].wait_recv()
        delta_copies[k].wait_recv()
    carried = jnp.zeros((modes, width), f32)
    prefix = carried
    for i in range(NZ):
        prefix = jnp.where(z == i, carried, prefix)
        carried = carried * block + lines[i] + late0 * delta[i, 0:1] + late1 * delta[i, 1:2]
    total[...] = carried
    own_sum[...] = prefix
    total_copies = {
        k: to_device(total, totals.at[x], total_send.at[k], total_recv.at[k], me + k * NZ)
        for k in range(1, NX)
    }
    for k in range(1, NX):
        pl.when(x + k < NX)(total_copies[k].start)

    far_sum[...] = jnp.zeros((modes, width), f32)
    for i in range(NX - 1):

        @pl.when(x > i)
        def _(i=i):
            to_device(total, totals.at[i], total_send.at[0], total_recv.at[x - i], me).wait_recv()
            far_sum[...] = far_sum[...] * hop + totals[i]

    state = own_sum[...] + jnp.exp(-decay[...] * (rows * z.astype(f32))) * far_sum[...]

    span = 256
    grow = lax.broadcasted_iota(jnp.int32, (span, span), 0) // modes
    gcol = lax.broadcasted_iota(jnp.int32, (span, span), 1) // size
    for u in range(width // span):
        cols = slice(u * span, (u + 1) * span)
        part = state[:, cols]
        blocks = jnp.where(grow == gcol, jnp.concatenate([part] * (span // modes), axis=0), 0.0)
        hi, lo = split(blocks)
        lh, ll = lead_hi[:, cols], lead_lo[:, cols]
        add = jnp.dot(lh, hi, preferred_element_type=f32)
        add += jnp.dot(lh, lo, preferred_element_type=f32)
        add += jnp.dot(ll, hi, preferred_element_type=f32)
        for i in range(span // LANES):
            t = u * (span // LANES) + i
            part = add[:, i * LANES : (i + 1) * LANES]
            out[:, t * LANES : (t + 1) * LANES] = (base[t] + qs[t] * part).astype(jnp.bfloat16)

    pl.when(me < last)(rim_copy.wait_send)
    for k in range(1, NZ):
        line_copies[k].wait_send()
        delta_copies[k].wait_send()
    for k in range(1, NX):
        pl.when(x + k < NX)(total_copies[k].wait_send)


def body(query_in, key_in, value_in, residues, decay_rate, short_filter, skip_gain):
    rows, width = query_in.shape
    modes = residues.shape[0]
    f32 = jnp.float32
    vmem = lambda *shape, dtype=f32: pltpu.VMEM(shape, dtype)
    dma = pltpu.SemaphoreType.DMA
    anywhere = pl.BlockSpec(memory_space=pl.ANY)
    return pl.pallas_call(
        kernel,
        out_shape=jax.ShapeDtypeStruct((rows, width), jnp.bfloat16),
        in_specs=[anywhere] * 7,
        out_specs=pl.BlockSpec(memory_space=pltpu.VMEM),
        scratch_shapes=[
            vmem(3, rows, width, dtype=jnp.bfloat16),
            vmem(3, width // LANES, FRONT + rows, LANES),
            vmem(*residues.shape),
            vmem(*decay_rate.shape),
            vmem(*short_filter.shape),
            vmem(*skip_gain.shape),
            vmem(modes, width),
            vmem(modes, width),
            vmem(rows, width),
            vmem(modes, SEGS, width),
            vmem(width // LANES, rows, LANES),
            vmem(width // LANES, rows, LANES),
            vmem(rows, width, dtype=jnp.bfloat16),
            vmem(rows, width, dtype=jnp.bfloat16),
            vmem(modes, width),
            vmem(NZ, modes, width),
            vmem(8, width),
            vmem(8, width),
            vmem(2, width),
            vmem(NZ, 2, width),
            vmem(modes, width),
            vmem(NX, modes, width),
            vmem(modes, width),
            vmem(modes, width),
            dma((7,)),
            dma((NZ,)), dma((NZ,)),
            dma((NZ,)), dma((NZ,)),
            dma((NX,)), dma((NX,)),
            dma, dma,
        ],
        compiler_params=pltpu.CompilerParams(
            collective_id=0, has_side_effects=True, vmem_limit_bytes=40 * 2**20
        ),
    )(query_in, key_in, value_in, residues, decay_rate, short_filter, skip_gain)


def solution(mesh):
    placed = (
        P("ctx", "fsdp"),
        P("ctx", "fsdp"),
        P("ctx", "fsdp"),
        P(None, "fsdp"),
        P(None, "fsdp"),
        P(None, None, "fsdp"),
        P(None, "fsdp"),
    )
    return jax.shard_map(
        body, mesh=mesh, in_specs=placed, out_specs=P("ctx", "fsdp"), check_vma=False
    )
```

```python
import functools

import jax
import jax.numpy as jnp
from jax import lax
from jax.experimental import pallas as pl
from jax.experimental.pallas import tpu as pltpu
from jax.sharding import PartitionSpec as P

MESH = pl.DeviceIdType.MESH
NX, NZ = 4, 8
SEGS = 8
LANES = 128
FRONT = 8


def to_device(src, dst, send, recv, ctx):
    return pltpu.make_async_remote_copy(
        src_ref=src,
        dst_ref=dst,
        send_sem=send,
        recv_sem=recv,
        device_id={"ctx": ctx},
        device_id_type=MESH,
    )


def one_minus_exp(u):
    series = u * (1 - u / 2 * (1 - u / 3 * (1 - u / 4 * (1 - u / 5 * (1 - u / 6 * (1 - u / 7))))))
    return jnp.where(u < 0.3, series, 1 - jnp.exp(-u))


def scan_segments(value, powers, row):
    for power, step in zip(powers, (1, 2, 4)):
        value = value + power * jnp.where(row >= step, pltpu.roll(value, step, 0), 0.0)
    return value


def split(x):
    high = x.astype(jnp.bfloat16)
    return high, (x - high.astype(jnp.float32)).astype(jnp.bfloat16)


def kernel(
    query, key, value, residues, decay_rate, short_filter, skip_gain,
    out,
    raw, wide, params_r, params_d, filt, skip,
    decay, weight, gated, final, base, qs, lead_hi, lead_lo,
    fresh, lines, edge, rim, delta_own, delta, total, totals, own_sum, far_sum,
    in_sem, line_send, line_recv, delta_send, delta_recv, total_send, total_recv, rim_send, rim_recv,
):
    rows, width = query.shape
    modes, groups = residues.shape
    size = width // groups
    steps = rows // SEGS
    tiles = width // LANES
    f32 = jnp.float32

    me = lax.axis_index("ctx")
    x, z = me // NZ, lax.rem(me, NZ)

    def line_peer(k):
        return x * NZ + lax.rem(z + k, NZ)

    barrier = pltpu.get_barrier_semaphore()

    def here(ctx):
        pl.semaphore_signal(barrier, inc=1, device_id={"ctx": ctx}, device_id_type=MESH)

    for k in range(1, NZ):
        here(line_peer(k))
    for k in range(1, NX):
        pl.when(x >= k)(functools.partial(here, me - k * NZ))
    pl.when((z == 0) & (x > 0))(functools.partial(here, me - 1))

    small = [
        pltpu.make_async_copy(a, b, in_sem.at[i])
        for i, (a, b) in enumerate(
            ((residues, params_r), (decay_rate, params_d), (short_filter, filt), (skip_gain, skip))
        )
    ]
    large = [
        pltpu.make_async_copy(a, raw.at[p], in_sem.at[4 + p])
        for p, a in enumerate((query, key, value))
    ]
    for copy in (small[1], small[0], small[2], large[1], large[2], large[0], small[3]):
        copy.start()

    small[0].wait()
    small[1].wait()
    small[2].wait()
    lane = lax.broadcasted_iota(jnp.int32, (groups, width), 1)
    group = lax.broadcasted_iota(jnp.int32, (groups, width), 0)
    pick = (lane // size == group).astype(f32)
    high = lax.Precision.HIGHEST
    rate = jnp.dot(params_d[...], pick, precision=high, preferred_element_type=f32)
    decay[...] = rate
    residue = jnp.dot(params_r[...], pick, precision=high, preferred_element_type=f32)
    weight[...] = residue * jnp.sqrt(one_minus_exp(2.0 * rate))

    row = lax.broadcasted_iota(jnp.int32, (SEGS, LANES), 0)

    def widen(p):
        for t in range(tiles):
            wide[p, t, 0:FRONT] = jnp.zeros((FRONT, LANES), f32)
            wide[p, t, FRONT:] = raw[p, :, t * LANES : (t + 1) * LANES].astype(f32)

    large[1].wait()
    widen(1)
    large[2].wait()
    widen(2)

    def segments(p, offset, tile):
        return wide[p, tile, pl.ds(FRONT + offset, SEGS, stride=steps)]

    def taps_of(p, cols):
        return [jnp.broadcast_to(filt[p, i : i + 1, cols], (SEGS, LANES)) for i in range(3)]

    def short(taps, now, last, older):
        return taps[0] * now + taps[1] * last + taps[2] * older

    for tile in range(tiles):
        cols = slice(tile * LANES, (tile + 1) * LANES)
        ktaps, vtaps = taps_of(1, cols), taps_of(2, cols)
        rates = [
            jnp.broadcast_to(jnp.exp(-decay[n : n + 1, cols]), (SEGS, LANES)) for n in range(modes)
        ]

        def advance(j, carry, tile=tile, cols=cols, ktaps=ktaps, vtaps=vtaps, rates=rates):
            k1, k2, v1, v2, states = carry
            k0, v0 = segments(1, j, tile), segments(2, j, tile)
            g = short(ktaps, k0, k1, k2) * short(vtaps, v0, v1, v2)
            gated[pl.ds(pl.multiple_of(j * SEGS, SEGS), SEGS), cols] = g
            states = tuple(s * a + g for s, a in zip(states, rates))
            return k0, k1, v0, v1, states

        zero = jnp.zeros((SEGS, LANES), f32)
        first = (
            segments(1, -1, tile), segments(1, -2, tile),
            segments(2, -1, tile), segments(2, -2, tile),
            (zero,) * modes,
        )
        states = lax.fori_loop(0, steps, advance, first, unroll=4)[4]
        for n in range(modes):
            final[n, :, cols] = states[n]
            powers = [jnp.exp(-decay[n : n + 1, cols] * (steps * s)) for s in (1, 2, 4)]
            fresh[n : n + 1, cols] = scan_segments(states[n], powers, row)[SEGS - 1 : SEGS]

    large[0].wait()
    for p in range(3):
        edge[2 * p : 2 * p + 2] = raw[p, rows - 8 : rows].astype(f32)[6:8]
    pl.semaphore_wait(
        barrier, NZ - 1 + NX - 1 - x + jnp.where((z == NZ - 1) & (x < NX - 1), 1, 0)
    )
    last = NX * NZ - 1
    rim_copy = to_device(edge, rim, rim_send, rim_recv, me + 1)
    pl.when(me < last)(rim_copy.start)
    line_copies = {
        k: to_device(fresh, lines.at[z], line_send.at[k], line_recv.at[k], line_peer(k))
        for k in range(1, NZ)
    }
    for k in (4, 3, 5, 2, 6, 1, 7):
        line_copies[k].start()
    lines[z] = fresh[...]

    lane = lax.broadcasted_iota(jnp.int32, (modes, width), 1)
    mode = lax.broadcasted_iota(jnp.int32, (modes, width), 0)
    own = lax.rem(lane, modes) == mode
    flat_rate = jnp.sum(jnp.where(own, decay[...], 0.0), axis=0, keepdims=True)
    flat_weight = jnp.sum(jnp.where(own, weight[...], 0.0), axis=0, keepdims=True)
    for tile in range(tiles):
        cols = slice(tile * LANES, (tile + 1) * LANES)
        rate8 = jnp.broadcast_to(flat_rate[:, cols], (16, LANES))
        row16 = lax.broadcasted_iota(jnp.int32, (16, LANES), 0).astype(f32)
        begin = flat_weight[:, cols] * jnp.exp(-rate8 * (row16 + 1.0))
        jump = jnp.exp(-rate8 * 16.0)

        def lead_rows(i, now, cols=cols, jump=jump):
            at = pl.ds(pl.multiple_of(i * 16, 16), 16)
            hi, lo = split(now)
            lead_hi[at, cols] = hi
            lead_lo[at, cols] = lo
            return now * jump

        lax.fori_loop(0, rows // 16, lead_rows, begin, unroll=4)
    widen(0)
    small[3].wait()

    @pl.when(me == 0)
    def _():
        rim[...] = jnp.zeros_like(rim)

    pl.when(me > 0)(rim_copy.wait_recv)
    for tile in range(tiles):
        cols = slice(tile * LANES, (tile + 1) * LANES)
        for p in range(3):
            wide[p, tile, FRONT - 2 : FRONT] = rim[2 * p : 2 * p + 2, cols]

        def head(p, tile=tile, cols=cols):
            front = wide[p, tile, FRONT - 2 : FRONT + 2]
            return sum(filt[p, i : i + 1, cols] * front[2 - i : 4 - i] for i in range(3))

        true_head = head(1) * head(2)
        for i in range(2):
            at = slice(i * SEGS, i * SEGS + 1)
            delta_own[i : i + 1, cols] = true_head[i : i + 1] - gated[at, cols]
            gated[at, cols] = true_head[i : i + 1]
    delta_copies = {
        k: to_device(delta_own, delta.at[z], delta_send.at[k], delta_recv.at[k], line_peer(k))
        for k in range(1, NZ)
    }
    for k in (4, 3, 5, 2, 6, 1, 7):
        delta_copies[k].start()
    delta[z] = delta_own[...]

    for tile in range(tiles):
        cols = slice(tile * LANES, (tile + 1) * LANES)
        qtaps = taps_of(0, cols)
        gain = jnp.broadcast_to(skip[0:1, cols], (SEGS, LANES))
        d0, d1 = delta_own[0:1, cols], delta_own[1:2, cols]
        rates, weights, entering = [], [], []
        for n in range(modes):
            rate = decay[n : n + 1, cols]
            powers = [jnp.exp(-rate * (steps * s)) for s in (1, 2, 4)]
            extra = jnp.exp(-rate * (steps - 1.0)) * d0 + jnp.exp(-rate * (steps - 2.0)) * d1
            state = final[n, :, cols] + jnp.where(row == 0, extra, 0.0)
            state = scan_segments(state, powers, row)
            entering.append(jnp.where(row >= 1, pltpu.roll(state, 1, 0), 0.0))
            rates.append(jnp.broadcast_to(jnp.exp(-rate), (SEGS, LANES)))
            weights.append(jnp.broadcast_to(weight[n : n + 1, cols], (SEGS, LANES)))

        def respond(j, carry, tile=tile, cols=cols, qtaps=qtaps, gain=gain, rates=rates, weights=weights):
            q1, q2, states = carry
            q0 = segments(0, j, tile)
            g = gated[pl.ds(pl.multiple_of(j * SEGS, SEGS), SEGS), cols]
            states = tuple(s * a + g for s, a in zip(states, rates))
            terms = [s * w for s, w in zip(states, weights)] + [gain * g]
            while len(terms) > 1:
                terms = [sum(terms[i : i + 2]) for i in range(0, len(terms), 2)]
            q = short(qtaps, q0, q1, q2)
            at = pl.ds(j, SEGS, stride=steps)
            base[tile, at] = q * terms[0]
            qs[tile, at] = q
            return q0, q1, states

        first = (segments(0, -1, tile), segments(0, -2, tile), tuple(entering))
        lax.fori_loop(0, steps, respond, first, unroll=4)

    block = jnp.exp(-decay[...] * rows)
    late0 = jnp.exp(-decay[...] * (rows - 1.0))
    late1 = jnp.exp(-decay[...] * (rows - 2.0))
    hop = jnp.exp(-decay[...] * (rows * NZ))
    for k in range(1, NZ):
        line_copies[k].wait_recv()
        delta_copies[k].wait_recv()
    carried = jnp.zeros((modes, width), f32)
    prefix = carried
    for i in range(NZ):
        prefix = jnp.where(z == i, carried, prefix)
        carried = carried * block + lines[i] + late0 * delta[i, 0:1] + late1 * delta[i, 1:2]
    total[...] = carried
    own_sum[...] = prefix
    total_copies = {
        k: to_device(total, totals.at[x], total_send.at[k], total_recv.at[k], me + k * NZ)
        for k in range(1, NX)
    }
    for k in range(1, NX):
        pl.when(x + k < NX)(total_copies[k].start)

    far_sum[...] = jnp.zeros((modes, width), f32)
    for i in range(NX - 1):

        @pl.when(x > i)
        def _(i=i):
            to_device(total, totals.at[i], total_send.at[0], total_recv.at[x - i], me).wait_recv()
            far_sum[...] = far_sum[...] * hop + totals[i]

    state = own_sum[...] + jnp.exp(-decay[...] * (rows * z.astype(f32))) * far_sum[...]

    span = 256
    grow = lax.broadcasted_iota(jnp.int32, (span, span), 0) // modes
    gcol = lax.broadcasted_iota(jnp.int32, (span, span), 1) // size
    for u in range(width // span):
        cols = slice(u * span, (u + 1) * span)
        part = state[:, cols]
        blocks = jnp.where(grow == gcol, jnp.concatenate([part] * (span // modes), axis=0), 0.0)
        hi, lo = split(blocks)
        lh, ll = lead_hi[:, cols], lead_lo[:, cols]
        add = jnp.dot(lh, hi, preferred_element_type=f32)
        add += jnp.dot(lh, lo, preferred_element_type=f32)
        add += jnp.dot(ll, hi, preferred_element_type=f32)
        for i in range(span // LANES):
            t = u * (span // LANES) + i
            part = add[:, i * LANES : (i + 1) * LANES]
            out[:, t * LANES : (t + 1) * LANES] = (base[t] + qs[t] * part).astype(jnp.bfloat16)

    pl.when(me < last)(rim_copy.wait_send)
    for k in range(1, NZ):
        line_copies[k].wait_send()
        delta_copies[k].wait_send()
    for k in range(1, NX):
        pl.when(x + k < NX)(total_copies[k].wait_send)


def body(query_in, key_in, value_in, residues, decay_rate, short_filter, skip_gain):
    rows, width = query_in.shape
    modes = residues.shape[0]
    f32 = jnp.float32
    vmem = lambda *shape, dtype=f32: pltpu.VMEM(shape, dtype)
    dma = pltpu.SemaphoreType.DMA
    hbm = pl.BlockSpec(memory_space=pltpu.HBM)
    return pl.pallas_call(
        kernel,
        out_shape=jax.ShapeDtypeStruct((rows, width), jnp.bfloat16),
        in_specs=[hbm] * 7,
        out_specs=pl.BlockSpec(memory_space=pltpu.VMEM),
        scratch_shapes=[
            vmem(3, rows, width, dtype=jnp.bfloat16),
            vmem(3, width // LANES, FRONT + rows, LANES),
            vmem(*residues.shape),
            vmem(*decay_rate.shape),
            vmem(*short_filter.shape),
            vmem(*skip_gain.shape),
            vmem(modes, width),
            vmem(modes, width),
            vmem(rows, width),
            vmem(modes, SEGS, width),
            vmem(width // LANES, rows, LANES),
            vmem(width // LANES, rows, LANES),
            vmem(rows, width, dtype=jnp.bfloat16),
            vmem(rows, width, dtype=jnp.bfloat16),
            vmem(modes, width),
            vmem(NZ, modes, width),
            vmem(8, width),
            vmem(8, width),
            vmem(2, width),
            vmem(NZ, 2, width),
            vmem(modes, width),
            vmem(NX, modes, width),
            vmem(modes, width),
            vmem(modes, width),
            dma((7,)),
            dma((NZ,)), dma((NZ,)),
            dma((NZ,)), dma((NZ,)),
            dma((NX,)), dma((NX,)),
            dma, dma,
        ],
        compiler_params=pltpu.CompilerParams(
            collective_id=0, has_side_effects=True, vmem_limit_bytes=40 * 2**20
        ),
    )(
        *(
            pltpu.with_memory_space_constraint(a, pltpu.HBM)
            for a in (query_in, key_in, value_in, residues, decay_rate, short_filter, skip_gain)
        )
    )


def solution(mesh):
    placed = (
        P("ctx", "fsdp"),
        P("ctx", "fsdp"),
        P("ctx", "fsdp"),
        P(None, "fsdp"),
        P(None, "fsdp"),
        P(None, None, "fsdp"),
        P(None, "fsdp"),
    )
    return jax.shard_map(
        body, mesh=mesh, in_specs=placed, out_specs=P("ctx", "fsdp"), check_vma=False
    )
```

```python
import functools

import jax
import jax.numpy as jnp
from jax import lax
from jax.experimental import pallas as pl
from jax.experimental.pallas import tpu as pltpu
from jax.sharding import PartitionSpec as P

MESH = pl.DeviceIdType.MESH
NX, NZ = 4, 8
SEGS = 8
LANES = 128
FRONT = 8


def to_device(src, dst, send, recv, ctx):
    return pltpu.make_async_remote_copy(
        src_ref=src,
        dst_ref=dst,
        send_sem=send,
        recv_sem=recv,
        device_id={"ctx": ctx},
        device_id_type=MESH,
    )


def one_minus_exp(u):
    series = u * (1 - u / 2 * (1 - u / 3 * (1 - u / 4 * (1 - u / 5 * (1 - u / 6 * (1 - u / 7))))))
    return jnp.where(u < 0.3, series, 1 - jnp.exp(-u))


def scan_segments(value, powers, row):
    for power, step in zip(powers, (1, 2, 4)):
        value = value + power * jnp.where(row >= step, pltpu.roll(value, step, 0), 0.0)
    return value


def split(x):
    high = x.astype(jnp.bfloat16)
    return high, (x - high.astype(jnp.float32)).astype(jnp.bfloat16)


def kernel(
    query, key, value, residues, decay_rate, short_filter, skip_gain,
    out,
    raw, wide, params_r, params_d, filt, skip,
    decay, weight, gated, final, base, qs, lead_hi, lead_lo,
    fresh, lines, edge, rim, ends_own, ends, ends_wide, deltas, delta_own, delta_first, total, totals, own_sum, far_sum,
    in_sem, line_send, line_recv, ends_send, ends_recv, delta_send, delta_recv, total_send, total_recv, rim_send, rim_recv,
):
    rows, width = query.shape
    modes, groups = residues.shape
    size = width // groups
    steps = rows // SEGS
    tiles = width // LANES
    f32 = jnp.float32

    me = lax.axis_index("ctx")
    x, z = me // NZ, lax.rem(me, NZ)

    others = [i + jnp.where(i >= z, 1, 0) for i in range(NZ - 1)]
    inner = x < NX - 1

    barrier = pltpu.get_barrier_semaphore()

    def here(ctx):
        pl.semaphore_signal(barrier, inc=1, device_id={"ctx": ctx}, device_id_type=MESH)

    for t in others:
        pl.when(inner | (t < z))(functools.partial(here, x * NZ + t))
    for k in range(1, NX):
        pl.when(x >= k)(functools.partial(here, me - k * NZ))
    pl.when((z == 0) & (x > 0))(functools.partial(here, me - 1))

    small = [
        pltpu.make_async_copy(a, b, in_sem.at[i])
        for i, (a, b) in enumerate(
            ((residues, params_r), (decay_rate, params_d), (short_filter, filt), (skip_gain, skip))
        )
    ]
    large = [
        pltpu.make_async_copy(a, raw.at[p], in_sem.at[4 + p])
        for p, a in enumerate((query, key, value))
    ]
    for copy in (small[1], small[0], small[2], large[1], large[2], large[0], small[3]):
        copy.start()

    small[0].wait()
    small[1].wait()
    small[2].wait()
    lane = lax.broadcasted_iota(jnp.int32, (groups, width), 1)
    group = lax.broadcasted_iota(jnp.int32, (groups, width), 0)
    pick = (lane // size == group).astype(f32)
    high = lax.Precision.HIGHEST
    rate = jnp.dot(params_d[...], pick, precision=high, preferred_element_type=f32)
    decay[...] = rate
    residue = jnp.dot(params_r[...], pick, precision=high, preferred_element_type=f32)
    weight[...] = residue * jnp.sqrt(one_minus_exp(2.0 * rate))

    row = lax.broadcasted_iota(jnp.int32, (SEGS, LANES), 0)

    def widen(p):
        for t in range(tiles):
            wide[p, t, 0:FRONT] = jnp.zeros((FRONT, LANES), f32)
            wide[p, t, FRONT:] = raw[p, :, t * LANES : (t + 1) * LANES].astype(f32)

    large[1].wait()
    widen(1)
    large[2].wait()
    widen(2)

    def segments(p, offset, tile):
        return wide[p, tile, pl.ds(FRONT + offset, SEGS, stride=steps)]

    def taps_of(p, cols):
        return [jnp.broadcast_to(filt[p, i : i + 1, cols], (SEGS, LANES)) for i in range(3)]

    def short(taps, now, last, older):
        return taps[0] * now + taps[1] * last + taps[2] * older

    zero = jnp.zeros((SEGS, LANES), f32)

    def pass_a(tile):
        cols = slice(tile * LANES, (tile + 1) * LANES)
        ktaps, vtaps = taps_of(1, cols), taps_of(2, cols)
        rates = [
            jnp.broadcast_to(jnp.exp(-decay[n : n + 1, cols]), (SEGS, LANES)) for n in range(modes)
        ]

        def advance(j, carry):
            k1, k2, v1, v2, states = carry
            k0, v0 = segments(1, j, tile), segments(2, j, tile)
            g = short(ktaps, k0, k1, k2) * short(vtaps, v0, v1, v2)
            gated[pl.ds(pl.multiple_of(j * SEGS, SEGS), SEGS), cols] = g
            states = tuple(s * a + g for s, a in zip(states, rates))
            return k0, k1, v0, v1, states

        first = (
            segments(1, -1, tile), segments(1, -2, tile),
            segments(2, -1, tile), segments(2, -2, tile),
            (zero,) * modes,
        )
        states = lax.fori_loop(0, steps, advance, first, unroll=4)[4]
        for n in range(modes):
            powers = [jnp.exp(-decay[n : n + 1, cols] * (steps * s)) for s in (1, 2, 4)]
            state = scan_segments(states[n], powers, row)
            final[n, :, cols] = state
            fresh[n : n + 1, cols] = state[SEGS - 1 : SEGS]

    pass_a(0)
    pass_a(1)

    large[0].wait()
    for tile in range(tiles):
        parts = []
        for p in (1, 2):
            parts.append(wide[p, tile, FRONT : FRONT + 2])
            parts.append(wide[p, tile, FRONT + rows - 2 : FRONT + rows])
        cols = slice(tile * LANES, (tile + 1) * LANES)
        ends_own[:, cols] = jnp.concatenate(parts, axis=0).astype(jnp.bfloat16)
    ends[z] = ends_own[...]
    for p in range(3):
        edge[2 * p : 2 * p + 2] = raw[p, rows - 8 : rows].astype(f32)[6:8]
    line_count = jnp.where(inner, NZ - 1, NZ - 1 - z)
    next_line = jnp.where((z == NZ - 1) & inner, 1, 0)
    last = NX * NZ - 1

    @pl.when(me < last)
    def _():
        pl.semaphore_wait(barrier, line_count + NX - 1 - x + next_line)

    rim_copy = to_device(edge, rim, rim_send, rim_recv, me + 1)
    pl.when(me < last)(rim_copy.start)

    def ends_line(t, source):
        return to_device(
            ends_own, ends.at[source], ends_send.at[t], ends_recv.at[source], x * NZ + t
        )

    for t in others:
        pl.when(inner | (t > z))(ends_line(t, z).start)

    pass_a(2)
    pass_a(3)

    line_copies = [
        to_device(fresh, lines.at[z], line_send.at[t], line_recv.at[z], x * NZ + t) for t in others
    ]
    for t, copy in zip(others, line_copies):
        pl.when(inner | (t > z))(copy.start)
    lines[z] = fresh[...]

    lane = lax.broadcasted_iota(jnp.int32, (modes, width), 1)
    mode = lax.broadcasted_iota(jnp.int32, (modes, width), 0)
    own = lax.rem(lane, modes) == mode
    flat_rate = jnp.sum(jnp.where(own, decay[...], 0.0), axis=0, keepdims=True)
    flat_weight = jnp.sum(jnp.where(own, weight[...], 0.0), axis=0, keepdims=True)
    for tile in range(tiles):
        cols = slice(tile * LANES, (tile + 1) * LANES)
        rate8 = jnp.broadcast_to(flat_rate[:, cols], (16, LANES))
        row16 = lax.broadcasted_iota(jnp.int32, (16, LANES), 0).astype(f32)
        begin = flat_weight[:, cols] * jnp.exp(-rate8 * (row16 + 1.0))
        jump = jnp.exp(-rate8 * 16.0)

        def lead_rows(i, now, cols=cols, jump=jump):
            at = pl.ds(pl.multiple_of(i * 16, 16), 16)
            hi, lo = split(now)
            lead_hi[at, cols] = hi
            lead_lo[at, cols] = lo
            return now * jump

        lax.fori_loop(0, rows // 16, lead_rows, begin, unroll=4)
    widen(0)
    small[3].wait()

    def head(p, tile, cols):
        front = jnp.concatenate([rim[2 * p : 2 * p + 2, cols], wide[p, tile, FRONT : FRONT + 2]], 0)
        return sum(filt[p, i : i + 1, cols] * front[2 - i : 4 - i] for i in range(3))

    def delta_line(t):
        return to_device(delta_own, delta_first, delta_send.at[t], delta_recv, x * NZ + t)

    def take_rim():
        @pl.when(me == 0)
        def _():
            rim[...] = jnp.zeros_like(rim)

        pl.when(me > 0)(rim_copy.wait_recv)
        for tile in range(tiles):
            cols = slice(tile * LANES, (tile + 1) * LANES)
            true_head = head(1, tile, cols) * head(2, tile, cols)
            for i in range(2):
                at = slice(i * SEGS, i * SEGS + 1)
                delta_own[i : i + 1, cols] = true_head[i : i + 1] - gated[at, cols]

        @pl.when(z == 0)
        def _():
            for t in range(1, NZ):
                delta_line(t).start()
            delta_first[...] = delta_own[...]

    def pass_b(tile):
        cols = slice(tile * LANES, (tile + 1) * LANES)
        qtaps = taps_of(0, cols)
        gain = jnp.broadcast_to(skip[0:1, cols], (SEGS, LANES))
        rates, weights, entering = [], [], []
        for n in range(modes):
            entering.append(jnp.where(row >= 1, pltpu.roll(final[n, :, cols], 1, 0), 0.0))
            rates.append(jnp.broadcast_to(jnp.exp(-decay[n : n + 1, cols]), (SEGS, LANES)))
            weights.append(jnp.broadcast_to(weight[n : n + 1, cols], (SEGS, LANES)))

        def respond(j, carry):
            q1, q2, states = carry
            q0 = segments(0, j, tile)
            g = gated[pl.ds(pl.multiple_of(j * SEGS, SEGS), SEGS), cols]
            states = tuple(s * a + g for s, a in zip(states, rates))
            terms = [s * w for s, w in zip(states, weights)] + [gain * g]
            while len(terms) > 1:
                terms = [sum(terms[i : i + 2]) for i in range(0, len(terms), 2)]
            at = pl.ds(j, SEGS, stride=steps)
            base[tile, at] = terms[0]
            qs[tile, at] = short(qtaps, q0, q1, q2)
            return q0, q1, states

        first = (segments(0, -1, tile), segments(0, -2, tile), tuple(entering))
        lax.fori_loop(0, steps, respond, first, unroll=4)

    pass_b(0)
    pass_b(1)
    pl.when(z == 0)(take_rim)
    pass_b(2)
    pass_b(3)
    pl.when(z > 0)(take_rim)

    d0, d1 = delta_own[0:1], delta_own[1:2]
    inverse = jnp.exp(decay[...])
    rim_state = inverse * (d0 + inverse * d1)
    excess = jnp.sum(weight[...] * inverse, axis=0, keepdims=True) * d1
    for tile in range(tiles):
        cols = slice(tile * LANES, (tile + 1) * LANES)
        base[tile, 0:1] += skip[0:1, cols] * d0[:, cols] - excess[:, cols]
        base[tile, 1:2] += skip[0:1, cols] * d1[:, cols]
        qs[tile, 0:2] = head(0, tile, cols)

    block = jnp.exp(-decay[...] * rows)
    late0 = jnp.exp(-decay[...] * (rows - 1.0))
    late1 = jnp.exp(-decay[...] * (rows - 2.0))
    hop = jnp.exp(-decay[...] * (rows * NZ))
    for t in others:
        pl.when(inner | (t < z))(ends_line(0, t).wait_recv)

    for t in range(NZ):
        for tile in range(tiles):
            part = ends[t, :, tile * LANES : (tile + 1) * LANES]
            ends_wide[tile, 8 * t : 8 * t + 8] = part.astype(f32)
    for tile in range(tiles):
        cols = slice(tile * LANES, (tile + 1) * LANES)
        olds, news = [], []
        for p in (1, 2):
            first, second, before2, before1 = [
                ends_wide[tile, pl.ds(4 * p - 4 + i, NZ, stride=8)] for i in range(4)
            ]
            before1, before2 = pltpu.roll(before1, 1, 0), pltpu.roll(before2, 1, 0)
            now, last1, last2 = [filt[p, i : i + 1, cols] for i in range(3)]
            old0, old1 = now * first, now * second + last1 * first
            olds.append((old0, old1))
            news.append((old0 + last1 * before1 + last2 * before2, old1 + last2 * before1))
        for i in range(2):
            deltas[i, :, cols] = news[0][i] * news[1][i] - olds[0][i] * olds[1][i]

    pl.when(z > 0)(delta_line(0).wait_recv)
    for t in others:

        @pl.when(inner | (t < z))
        def _(t=t):
            to_device(fresh, lines.at[t], line_send.at[t], line_recv.at[t], me).wait_recv()

    carried = jnp.zeros((modes, width), f32)
    prefix = carried
    for i in range(NZ):
        prefix = jnp.where(z == i, carried, prefix)
        e0, e1 = [deltas[j, i : i + 1] if i else delta_first[j : j + 1] for j in range(2)]
        carried = carried * block + lines[i] + late0 * e0 + late1 * e1
    total[...] = carried
    own_sum[...] = prefix + rim_state
    total_copies = {
        k: to_device(total, totals.at[x], total_send.at[k], total_recv.at[k], me + k * NZ)
        for k in range(1, NX)
    }
    for k in range(1, NX):
        pl.when(x + k < NX)(total_copies[k].start)

    far_sum[...] = jnp.zeros((modes, width), f32)
    for i in range(NX - 1):

        @pl.when(x > i)
        def _(i=i):
            to_device(total, totals.at[i], total_send.at[0], total_recv.at[x - i], me).wait_recv()
            far_sum[...] = far_sum[...] * hop + totals[i]

    state = own_sum[...] + jnp.exp(-decay[...] * (rows * z.astype(f32))) * far_sum[...]

    span = 256
    grow = lax.broadcasted_iota(jnp.int32, (span, span), 0) // modes
    gcol = lax.broadcasted_iota(jnp.int32, (span, span), 1) // size
    for u in range(width // span):
        cols = slice(u * span, (u + 1) * span)
        part = state[:, cols]
        blocks = jnp.where(grow == gcol, jnp.concatenate([part] * (span // modes), axis=0), 0.0)
        hi, lo = split(blocks)
        lh, ll = lead_hi[:, cols], lead_lo[:, cols]
        add = jnp.dot(lh, hi, preferred_element_type=f32)
        add += jnp.dot(lh, lo, preferred_element_type=f32)
        add += jnp.dot(ll, hi, preferred_element_type=f32)
        for i in range(span // LANES):
            t = u * (span // LANES) + i
            part = add[:, i * LANES : (i + 1) * LANES]
            out[:, t * LANES : (t + 1) * LANES] = (qs[t] * (base[t] + part)).astype(jnp.bfloat16)

    pl.when(me < last)(rim_copy.wait_send)
    for t, line_copy in zip(others, line_copies):

        @pl.when(inner | (t > z))
        def _(t=t, line_copy=line_copy):
            line_copy.wait_send()
            ends_line(t, z).wait_send()

    @pl.when(z == 0)
    def _():
        for t in range(1, NZ):
            delta_line(t).wait_send()

    for k in range(1, NX):
        pl.when(x + k < NX)(total_copies[k].wait_send)


def body(query_in, key_in, value_in, residues, decay_rate, short_filter, skip_gain):
    rows, width = query_in.shape
    modes, tiles = residues.shape[0], width // LANES
    f32 = jnp.float32
    vmem = lambda *shape, dtype=f32: pltpu.VMEM(shape, dtype)
    dma = pltpu.SemaphoreType.DMA
    hbm = pl.BlockSpec(memory_space=pltpu.HBM)
    return pl.pallas_call(
        kernel,
        out_shape=jax.ShapeDtypeStruct((rows, width), jnp.bfloat16),
        in_specs=[hbm] * 7,
        out_specs=pl.BlockSpec(memory_space=pltpu.VMEM),
        scratch_shapes=[
            vmem(3, rows, width, dtype=jnp.bfloat16),
            vmem(3, tiles, FRONT + rows, LANES),
            vmem(*residues.shape),
            vmem(*decay_rate.shape),
            vmem(*short_filter.shape),
            vmem(*skip_gain.shape),
            vmem(modes, width),
            vmem(modes, width),
            vmem(rows, width),
            vmem(modes, SEGS, width),
            vmem(tiles, rows, LANES),
            vmem(tiles, rows, LANES),
            vmem(rows, width, dtype=jnp.bfloat16),
            vmem(rows, width, dtype=jnp.bfloat16),
            vmem(modes, width),
            vmem(NZ, modes, width),
            vmem(8, width),
            vmem(8, width),
            vmem(8, width, dtype=jnp.bfloat16),
            vmem(NZ, 8, width, dtype=jnp.bfloat16),
            vmem(tiles, NZ * 8, LANES),
            vmem(2, NZ, width),
            vmem(2, width),
            vmem(2, width),
            vmem(modes, width),
            vmem(NX, modes, width),
            vmem(modes, width),
            vmem(modes, width),
            dma((7,)),
            dma((NZ,)), dma((NZ,)),
            dma((NZ,)), dma((NZ,)),
            dma((NZ,)), dma,
            dma((NX,)), dma((NX,)),
            dma, dma,
        ],
        compiler_params=pltpu.CompilerParams(
            collective_id=0, has_side_effects=True, vmem_limit_bytes=40 * 2**20
        ),
    )(
        *(
            pltpu.with_memory_space_constraint(a, pltpu.HBM)
            for a in (query_in, key_in, value_in, residues, decay_rate, short_filter, skip_gain)
        )
    )


def solution(mesh):
    placed = (
        P("ctx", "fsdp"),
        P("ctx", "fsdp"),
        P("ctx", "fsdp"),
        P(None, "fsdp"),
        P(None, "fsdp"),
        P(None, None, "fsdp"),
        P(None, "fsdp"),
    )
    return jax.shard_map(
        body, mesh=mesh, in_specs=placed, out_specs=P("ctx", "fsdp"), check_vma=False
    )
```

```python
import functools

import jax
import jax.numpy as jnp
from jax import lax
from jax.experimental import pallas as pl
from jax.experimental.pallas import tpu as pltpu
from jax.sharding import PartitionSpec as P

MESH = pl.DeviceIdType.MESH
NX, NZ = 4, 8
SEGS = 8
LANES = 128
FRONT = 8
LATE = NZ // 2
RELAY = LATE - 1
HALVES = 2


def to_device(src, dst, send, recv, ctx):
    return pltpu.make_async_remote_copy(
        src_ref=src,
        dst_ref=dst,
        send_sem=send,
        recv_sem=recv,
        device_id={"ctx": ctx},
        device_id_type=MESH,
    )


def one_minus_exp(u):
    series = u * (1 - u / 2 * (1 - u / 3 * (1 - u / 4 * (1 - u / 5 * (1 - u / 6 * (1 - u / 7))))))
    return jnp.where(u < 0.3, series, 1 - jnp.exp(-u))


def scan_segments(value, powers, row):
    for power, step in zip(powers, (1, 2, 4)):
        value = value + power * jnp.where(row >= step, pltpu.roll(value, step, 0), 0.0)
    return value


def split_f32(x):
    high = x.astype(jnp.bfloat16)
    return high, x - high.astype(jnp.float32)


def split(x):
    high, rest = split_f32(x)
    return high, rest.astype(jnp.bfloat16)


def kernel(
    query, key, value, residues, decay_rate, short_filter, skip_gain,
    out,
    raw, wide, params_r, params_d, filt, skip,
    decay, weight, gated, final, base, qs, lead_hi, lead_lo,
    fresh, lines, relayed, edge, rim, ends_own, ends, ends_wide, deltas, delta_own, total, totals, own_sum, far_sum,
    in_sem, line_send, line_recv, ends_send, ends_recv, tail_send, tail_recv, total_send, total_recv, rim_send, rim_recv,
    ready,
):
    rows, width = query.shape
    modes, groups = residues.shape
    size = width // groups
    steps = rows // SEGS
    tiles = width // LANES
    pitch = FRONT + steps
    part = width // HALVES
    f32 = jnp.float32

    me = lax.axis_index("ctx")
    x, z = me // NZ, lax.rem(me, NZ)

    inner = x < NX - 1

    early = z < LATE
    parity = lax.rem(z, 2)
    partner = 1 - 2 * parity

    def takes(half):
        return parity == half

    def sends_to(t):
        ahead = t > z
        if t >= LATE:
            ahead &= z >= RELAY
        return ahead | ((t < z) & inner)

    def hears_from(t):
        heard = (t < z) | ((t > z) & inner)
        return heard & early if t < RELAY else heard

    def sends_half(t, half):
        return sends_to(t) if half == t % 2 else sends_to(t) & (t > z)

    def hears_half(t, half):
        return hears_from(t) & ((t < z) | takes(half))

    barrier = pltpu.get_barrier_semaphore()

    def signal(sem, ctx):
        pl.semaphore_signal(sem, inc=1, device_id={"ctx": ctx}, device_id_type=MESH)

    for t in range(NZ):
        pl.when(hears_from(t))(functools.partial(signal, barrier, x * NZ + t))
    pl.when(early & (x > 0))(functools.partial(signal, barrier, x * NZ - 1))
    for k in range(1, NX):
        pl.when(x + k < NX)(functools.partial(signal, barrier, me + k * NZ))
        pl.when(x + k < NX)(functools.partial(signal, barrier, me + k * NZ + partner))

    small = [
        pltpu.make_async_copy(a, b, in_sem.at[i])
        for i, (a, b) in enumerate(
            ((residues, params_r), (decay_rate, params_d), (short_filter, filt), (skip_gain, skip))
        )
    ]
    large = [
        pltpu.make_async_copy(a, raw.at[p], in_sem.at[4 + p])
        for p, a in enumerate((query, key, value))
    ]
    for copy in (small[1], small[0], small[2], large[1], large[2], large[0], small[3]):
        copy.start()

    lane = lax.broadcasted_iota(jnp.int32, (groups, width), 1)
    group = lax.broadcasted_iota(jnp.int32, (groups, width), 0)
    pick = (lane // size == group).astype(f32).astype(jnp.bfloat16)
    pick = jnp.concatenate([pick] * 3, axis=0)

    def per_channel(values):
        high, rest = split_f32(values)
        middle, rest = split_f32(rest)
        parts = jnp.concatenate([high, middle, rest.astype(jnp.bfloat16)], axis=1)
        return jnp.dot(parts, pick, preferred_element_type=f32)

    small[1].wait()
    decay[...] = per_channel(params_d[...])
    row = lax.broadcasted_iota(jnp.int32, (SEGS, LANES), 0)

    def widen(p):
        for t in range(tiles):
            for i in range(SEGS):
                at = i * pitch + FRONT
                wide[p, t, at : at + steps] = raw[
                    p, i * steps : (i + 1) * steps, t * LANES : (t + 1) * LANES
                ].astype(f32)
                if i:
                    wide[p, t, at - FRONT : at] = wide[p, t, at - pitch + steps - FRONT : at - FRONT]
                else:
                    wide[p, t, 0:FRONT] = jnp.zeros((FRONT, LANES), f32)

    large[1].wait()
    widen(1)
    large[2].wait()
    widen(2)
    small[2].wait()

    def segments(p, offset, tile):
        return wide[p, tile, pl.ds(FRONT + offset, SEGS, stride=pitch)]

    def taps_of(p, cols):
        return [jnp.broadcast_to(filt[p, i : i + 1, cols], (SEGS, LANES)) for i in range(3)]

    def short(taps, now, last, older):
        return taps[0] * now + taps[1] * last + taps[2] * older

    zero = jnp.zeros((SEGS, LANES), f32)

    def pass_a(tile):
        cols = slice(tile * LANES, (tile + 1) * LANES)
        ktaps, vtaps = taps_of(1, cols), taps_of(2, cols)
        rates = [
            jnp.broadcast_to(jnp.exp(-decay[n : n + 1, cols]), (SEGS, LANES)) for n in range(modes)
        ]

        def advance(j, carry):
            k1, k2, v1, v2, states = carry
            k0, v0 = segments(1, j, tile), segments(2, j, tile)
            g = short(ktaps, k0, k1, k2) * short(vtaps, v0, v1, v2)
            gated[pl.ds(pl.multiple_of(j * SEGS, SEGS), SEGS), cols] = g
            states = tuple(s * a + g for s, a in zip(states, rates))
            return k0, k1, v0, v1, states

        first = (
            segments(1, -1, tile), segments(1, -2, tile),
            segments(2, -1, tile), segments(2, -2, tile),
            (zero,) * modes,
        )
        states = lax.fori_loop(0, steps, advance, first, unroll=4)[4]
        for n in range(modes):
            powers = [jnp.exp(-decay[n : n + 1, cols] * (steps * s)) for s in (1, 2, 4)]
            state = scan_segments(states[n], powers, row)
            final[n, :, cols] = state
            half, at = divmod(tile * LANES, part)
            fresh[half, n : n + 1, at : at + LANES] = state[SEGS - 1 : SEGS]

    pass_a(0)
    pass_a(1)

    large[0].wait()
    tail = []
    for tile in range(tiles):
        parts = []
        for p in (1, 2):
            parts.append(wide[p, tile, FRONT : FRONT + 2])
            parts.append(wide[p, tile, SEGS * pitch - 2 : SEGS * pitch])
        half, at = divmod(tile * LANES, part)
        ends_own[half, :, at : at + LANES] = jnp.concatenate(parts, axis=0).astype(jnp.bfloat16)
    ends[z] = ends_own[...]
    for p in range(3):
        tail.append(raw[p, rows - 8 : rows].astype(f32)[6:8])
    edge[...] = jnp.concatenate(tail + [jnp.zeros((2, width), f32)], axis=0).astype(jnp.bfloat16)
    last = NX * NZ - 1
    line_count = sum(jnp.where(sends_to(t), 1, 0) for t in range(NZ))
    ends_line_here = (z == NZ - 1) & inner
    pl.semaphore_wait(barrier, line_count + jnp.where(ends_line_here, LATE, 0) + 2 * x)
    for k in range(1, NX):
        pl.when(x >= k)(functools.partial(signal, ready, me - k * NZ))
        pl.when(x >= k)(functools.partial(signal, ready, me - k * NZ + partner))
    rim_copy = to_device(edge, rim, rim_send, rim_recv, me + 1)

    def tail_line(t):
        return to_device(ends_own, ends.at[NZ], tail_send.at[t], tail_recv, (x + 1) * NZ + t)

    @pl.when(ends_line_here)
    def _():
        for t in range(LATE):
            tail_line(t).start()

    def ends_line(t, source, half):
        return to_device(
            ends_own.at[half], ends.at[source, half],
            ends_send.at[t, half], ends_recv.at[source, half], x * NZ + t,
        )

    sooner, later = range(LATE), range(LATE, NZ)
    for half in range(HALVES):
        for t in sooner:
            pl.when(sends_half(t, half))(ends_line(t, z, half).start)

    def line_copy(t, source, half):
        return to_device(
            fresh.at[half], lines.at[source, half],
            line_send.at[t, half], line_recv.at[source, half], x * NZ + t,
        )

    def send_states(half):
        for t in sooner:
            pl.when(sends_half(t, half))(line_copy(t, z, half).start)
        lines[z, half] = fresh[half]

    send_states(0)
    pass_a(2)
    pass_a(3)
    send_states(1)

    small[0].wait()
    weight[...] = per_channel(params_r[...]) * jnp.sqrt(one_minus_exp(2.0 * decay[...]))

    lane = lax.broadcasted_iota(jnp.int32, (modes, width), 1)
    mode = lax.broadcasted_iota(jnp.int32, (modes, width), 0)
    own = lax.rem(lane, modes) == mode
    flat_rate = jnp.sum(jnp.where(own, decay[...], 0.0), axis=0, keepdims=True)
    flat_weight = jnp.sum(jnp.where(own, weight[...], 0.0), axis=0, keepdims=True)
    for tile in range(tiles):
        cols = slice(tile * LANES, (tile + 1) * LANES)
        rate8 = jnp.broadcast_to(flat_rate[:, cols], (16, LANES))
        row16 = lax.broadcasted_iota(jnp.int32, (16, LANES), 0).astype(f32)
        begin = flat_weight[:, cols] * jnp.exp(-rate8 * (row16 + 1.0))
        jump = jnp.exp(-rate8 * 16.0)

        def lead_rows(i, now, cols=cols, jump=jump):
            at = pl.ds(pl.multiple_of(i * 16, 16), 16)
            hi, lo = split(now)
            lead_hi[at, cols] = hi
            lead_lo[at, cols] = lo
            return now * jump

        lax.fori_loop(0, rows // 16, lead_rows, begin, unroll=4)
    pl.when(me < last)(rim_copy.start)
    for t in later:

        for half in range(HALVES):

            @pl.when(sends_half(t, half) & (z >= LATE))
            def _(t=t, half=half):
                ends_line(t, z, half).start()
                line_copy(t, z, half).start()

    widen(0)
    small[3].wait()

    def head(p, tile, cols):
        before = rim[:, cols].astype(f32)[2 * p : 2 * p + 2]
        front = jnp.concatenate([before, wide[p, tile, FRONT : FRONT + 2]], axis=0)
        return sum(filt[p, i : i + 1, cols] * front[2 - i : 4 - i] for i in range(3))

    def take_rim():
        @pl.when(me == 0)
        def _():
            rim[...] = jnp.zeros_like(rim)

        pl.when(me > 0)(rim_copy.wait_recv)
        for tile in range(tiles):
            cols = slice(tile * LANES, (tile + 1) * LANES)
            true_head = head(1, tile, cols) * head(2, tile, cols)
            for i in range(2):
                at = slice(i * SEGS, i * SEGS + 1)
                delta_own[i : i + 1, cols] = true_head[i : i + 1] - gated[at, cols]

    def pass_b(tile):
        cols = slice(tile * LANES, (tile + 1) * LANES)
        qtaps = taps_of(0, cols)
        gain = jnp.broadcast_to(skip[0:1, cols], (SEGS, LANES))
        rates, weights, entering = [], [], []
        for n in range(modes):
            entering.append(jnp.where(row >= 1, pltpu.roll(final[n, :, cols], 1, 0), 0.0))
            rates.append(jnp.broadcast_to(jnp.exp(-decay[n : n + 1, cols]), (SEGS, LANES)))
            weights.append(jnp.broadcast_to(weight[n : n + 1, cols], (SEGS, LANES)))

        def respond(j, carry):
            q1, q2, states = carry
            q0 = segments(0, j, tile)
            g = gated[pl.ds(pl.multiple_of(j * SEGS, SEGS), SEGS), cols]
            states = tuple(s * a + g for s, a in zip(states, rates))
            terms = [s * w for s, w in zip(states, weights)] + [gain * g]
            while len(terms) > 1:
                terms = [sum(terms[i : i + 2]) for i in range(0, len(terms), 2)]
            at = pl.ds(j, SEGS, stride=steps)
            base[tile, at] = terms[0]
            qs[tile, at] = short(qtaps, q0, q1, q2)
            return q0, q1, states

        first = (segments(0, -1, tile), segments(0, -2, tile), tuple(entering))
        lax.fori_loop(0, steps, respond, first, unroll=4)

    def corrections(known):
        for t in known:
            for tile in range(tiles):
                half, at = divmod(tile * LANES, part)
                piece = ends[t, half, :, at : at + LANES]
                ends_wide[tile, 8 * t : 8 * t + 8] = piece.astype(f32)
        for tile in range(tiles):
            cols = slice(tile * LANES, (tile + 1) * LANES)
            olds, news = [], []
            for p in (1, 2):
                first, second, before2, before1 = [
                    ends_wide[tile, pl.ds(4 * p - 4 + i, NZ, stride=8)] for i in range(4)
                ]
                line_before = jnp.where(x > 0, ends_wide[tile, 8 * NZ + 4 * p - 2 : 8 * NZ + 4 * p], 0.0)
                before2 = jnp.where(row == 0, line_before[0:1], pltpu.roll(before2, 1, 0))
                before1 = jnp.where(row == 0, line_before[1:2], pltpu.roll(before1, 1, 0))
                now, last1, last2 = [filt[p, i : i + 1, cols] for i in range(3)]
                old0, old1 = now * first, now * second + last1 * first
                olds.append((old0, old1))
                news.append((old0 + last1 * before1 + last2 * before2, old1 + last2 * before1))
            for i in range(2):
                deltas[i, :, cols] = news[0][i] * news[1][i] - olds[0][i] * olds[1][i]

    def own_factors(half):
        rate = decay[:, half * part : (half + 1) * part]
        return jnp.exp(-rate * rows), jnp.exp(-rate * (rows - 1.0)), jnp.exp(-rate * (rows - 2.0))

    def add_line(i, half, carried, block, late0, late1):
        cols = slice(half * part, (half + 1) * part)
        e0, e1 = [deltas[j, i : i + 1, cols] for j in range(2)]
        return carried * block + lines[i, half] + late0 * e0 + late1 * e1

    def relay_copy(t, half):
        return to_device(
            relayed.at[half], lines.at[RELAY, half],
            line_send.at[t, half], line_recv.at[RELAY, half], x * NZ + t,
        )

    def relay():
        for half in range(HALVES):
            for t in range(RELAY):
                ends_line(0, t, half).wait_recv()
                line_copy(0, t, half).wait_recv()
        pl.when(x > 0)(tail_line(0).wait_recv)
        corrections([*range(LATE), NZ])
        for half in range(HALVES):
            factors = own_factors(half)
            carried = jnp.zeros((modes, part), f32)
            for i in range(LATE):
                carried = add_line(i, half, carried, *factors)
            relayed[half] = carried
        for t in later:
            for half in range(HALVES):
                ends_line(t, z, half).start()
                relay_copy(t, half).start()

    pass_b(0)
    pass_b(1)
    pass_b(2)
    pl.when(z == RELAY)(relay)
    pass_b(3)

    pl.when((z < RELAY) & (x > 0))(tail_line(0).wait_recv)
    for half in range(HALVES):
        for t in range(NZ):
            heard = hears_half(t, half)
            if t < RELAY:
                heard &= z != RELAY
            pl.when(heard)(ends_line(0, t, half).wait_recv)

    corrections(range(NZ + 1))
    def total_copy(k, source, half, shift=0):
        way = 0 if isinstance(shift, int) else 1
        return to_device(
            total.at[half], totals.at[source, half],
            total_send.at[way, k, half], total_recv.at[source, half], me + k * NZ + shift,
        )

    def sum_line(half, upto=None):
        factors = own_factors(half)
        carried = jnp.zeros((modes, part), f32)
        for i in range(NZ):
            after = add_line(i, half, carried, *factors)
            if i == RELAY:
                after = jnp.where(early, after, lines[RELAY, half])
            carried = after if upto is None else jnp.where(upto > i, after, carried)
        return carried

    for half in range(HALVES):
        for t in range(NZ):
            heard = hears_half(t, half)
            if t < RELAY:
                heard &= z != RELAY
            pl.when(heard)(line_copy(0, t, half).wait_recv)

        @pl.when(takes(half) & inner)
        def _(half=half):
            total[half] = sum_line(half)

    pl.when(inner)(lambda: pl.semaphore_wait(ready, 2 * (NX - 1 - x)))
    for half in range(HALVES):
        for k in range(1, NX):
            pl.when((x + k < NX) & takes(half))(total_copy(k, x, half).start)
            pl.when((x + k < NX) & takes(half))(total_copy(k, x, half, partner).start)

    take_rim()
    d0, d1 = delta_own[0:1], delta_own[1:2]
    inverse = jnp.exp(decay[...])
    rim_state = inverse * (d0 + inverse * d1)
    excess = jnp.sum(weight[...] * inverse, axis=0, keepdims=True) * d1
    for tile in range(tiles):
        cols = slice(tile * LANES, (tile + 1) * LANES)
        base[tile, 0:1] += skip[0:1, cols] * d0[:, cols] - excess[:, cols]
        base[tile, 1:2] += skip[0:1, cols] * d1[:, cols]
        qs[tile, 0:2] = head(0, tile, cols)

    for half in range(HALVES):
        own_sum[half] = sum_line(half, z) + rim_state[:, half * part : (half + 1) * part]

    states = []
    for half in range(HALVES):
        rate = decay[:, half * part : (half + 1) * part]
        hop = jnp.exp(-rate * (rows * NZ))
        into_line = jnp.exp(-rate * (rows * z.astype(f32)))
        far_sum[...] = jnp.zeros_like(far_sum)
        for i in range(NX - 1):

            @pl.when(x > i)
            def _(i=i, half=half, hop=hop):
                total_copy(0, i, half).wait_recv()
                far_sum[...] = far_sum[...] * hop + totals[i, half]

        states.append(own_sum[half] + into_line * far_sum[...])

    grow = lax.broadcasted_iota(jnp.int32, (part, part), 0) // modes
    gcol = lax.broadcasted_iota(jnp.int32, (part, part), 1) // size
    for half in range(HALVES):
        cols = slice(half * part, (half + 1) * part)
        blocks = jnp.concatenate([states[half]] * (part // modes), axis=0)
        hi, lo = split(jnp.where(grow == gcol, blocks, 0.0))
        lh, ll = lead_hi[:, cols], lead_lo[:, cols]
        add = jnp.dot(lh, hi, preferred_element_type=f32)
        add += jnp.dot(lh, lo, preferred_element_type=f32)
        add += jnp.dot(ll, hi, preferred_element_type=f32)
        for t in range(half * part // LANES, (half + 1) * part // LANES):
            more = add[:, t * LANES - half * part : (t + 1) * LANES - half * part]
            out[:, t * LANES : (t + 1) * LANES] = (qs[t] * (base[t] + more)).astype(jnp.bfloat16)

    pl.when(me < last)(rim_copy.wait_send)
    for t in range(NZ):
        for half in range(HALVES):

            @pl.when(sends_half(t, half))
            def _(t=t, half=half):
                ends_line(t, z, half).wait_send()
                line_copy(t, z, half).wait_send()

    @pl.when(ends_line_here)
    def _():
        for t in range(LATE):
            tail_line(t).wait_send()

    for k in range(1, NX):

        @pl.when(x + k < NX)
        def _(k=k):
            for half in range(HALVES):
                pl.when(takes(half))(total_copy(k, x, half).wait_send)
                pl.when(takes(half))(total_copy(k, x, half, partner).wait_send)


def body(query_in, key_in, value_in, residues, decay_rate, short_filter, skip_gain):
    rows, width = query_in.shape
    modes, tiles = residues.shape[0], width // LANES
    pitched = FRONT * SEGS + rows
    half = (modes, width // HALVES)
    f32 = jnp.float32
    vmem = lambda *shape, dtype=f32: pltpu.VMEM(shape, dtype)
    dma = pltpu.SemaphoreType.DMA
    hbm = pl.BlockSpec(memory_space=pltpu.HBM)
    return pl.pallas_call(
        kernel,
        out_shape=jax.ShapeDtypeStruct((rows, width), jnp.bfloat16),
        in_specs=[hbm] * 7,
        out_specs=pl.BlockSpec(memory_space=pltpu.VMEM),
        scratch_shapes=[
            vmem(3, rows, width, dtype=jnp.bfloat16),
            vmem(3, tiles, pitched, LANES),
            vmem(*residues.shape),
            vmem(*decay_rate.shape),
            vmem(*short_filter.shape),
            vmem(*skip_gain.shape),
            vmem(modes, width),
            vmem(modes, width),
            vmem(rows, width),
            vmem(modes, SEGS, width),
            vmem(tiles, rows, LANES),
            vmem(tiles, rows, LANES),
            vmem(rows, width, dtype=jnp.bfloat16),
            vmem(rows, width, dtype=jnp.bfloat16),
            vmem(HALVES, *half),
            vmem(NZ, HALVES, *half),
            vmem(HALVES, *half),
            vmem(8, width, dtype=jnp.bfloat16),
            vmem(8, width, dtype=jnp.bfloat16),
            vmem(HALVES, 8, width // HALVES, dtype=jnp.bfloat16),
            vmem(NZ + 1, HALVES, 8, width // HALVES, dtype=jnp.bfloat16),
            vmem(tiles, NZ * 8 + 8, LANES),
            vmem(2, NZ, width),
            vmem(2, width),
            vmem(HALVES, *half),
            vmem(NX, HALVES, *half),
            vmem(HALVES, *half),
            vmem(*half),
            dma((7,)),
            dma((NZ, HALVES)), dma((NZ, HALVES)),
            dma((NZ, HALVES)), dma((NZ, HALVES)),
            dma((LATE,)), dma,
            dma((2, NX, HALVES)), dma((NX, HALVES)),
            dma, dma,
            pltpu.SemaphoreType.REGULAR,
        ],
        compiler_params=pltpu.CompilerParams(
            collective_id=0, has_side_effects=True, vmem_limit_bytes=40 * 2**20
        ),
    )(
        *(
            pltpu.with_memory_space_constraint(a, pltpu.HBM)
            for a in (query_in, key_in, value_in, residues, decay_rate, short_filter, skip_gain)
        )
    )


def solution(mesh):
    placed = (
        P("ctx", "fsdp"),
        P("ctx", "fsdp"),
        P("ctx", "fsdp"),
        P(None, "fsdp"),
        P(None, "fsdp"),
        P(None, None, "fsdp"),
        P(None, "fsdp"),
    )
    return jax.shard_map(
        body, mesh=mesh, in_specs=placed, out_specs=P("ctx", "fsdp"), check_vma=False
    )
```

```python
import functools

import jax
import jax.numpy as jnp
from jax import lax
from jax.experimental import pallas as pl
from jax.experimental.pallas import tpu as pltpu
from jax.sharding import PartitionSpec as P

MESH = pl.DeviceIdType.MESH
NX, NZ = 4, 8
SEGS = 8
LANES = 128
FRONT = 8
LATE = NZ // 2
RELAY = LATE - 1
HALVES = 2


def to_device(src, dst, send, recv, ctx):
    return pltpu.make_async_remote_copy(
        src_ref=src,
        dst_ref=dst,
        send_sem=send,
        recv_sem=recv,
        device_id={"ctx": ctx},
        device_id_type=MESH,
    )


def wait_for(semaphore, slots, count, most, send=False):
    for n in [count] if isinstance(count, int) else range(1, most + 1):
        some = slots.at[pl.ds(0, n)]
        copy = to_device(some, some, semaphore, semaphore, 0)
        pl.when(count == n)(copy.wait_send if send else copy.wait_recv)


def slot(source, half):
    return source * HALVES + half


def count_of(conditions):
    return sum(jnp.where(condition, 1, 0) for condition in conditions)


def one_minus_exp(u):
    series = u * (1 - u / 2 * (1 - u / 3 * (1 - u / 4 * (1 - u / 5 * (1 - u / 6 * (1 - u / 7))))))
    return jnp.where(u < 0.3, series, 1 - jnp.exp(-u))


def scan_segments(value, powers, row):
    for power, step in zip(powers, (1, 2, 4)):
        value = value + power * jnp.where(row >= step, pltpu.roll(value, step, 0), 0.0)
    return value


def split_f32(x):
    high = x.astype(jnp.bfloat16)
    return high, x - high.astype(jnp.float32)


def split(x):
    high, rest = split_f32(x)
    return high, rest.astype(jnp.bfloat16)


def kernel(
    query, key, value, residues, decay_rate, short_filter, skip_gain,
    out,
    raw, wide, params_r, params_d, filt, skip,
    decay, weight, gated, final, base, qs, lead_hi, lead_lo,
    fresh, lines, relayed, edge, rim, ends_own, ends, ends_wide, deltas, delta_own, total, totals, own_sum,
    small_sem, large_sem, line_send, line_recv, ends_send, ends_recv, tail_send, tail_recv, total_send, total_recv, rim_send, rim_recv,
    ready,
):
    rows, width = query.shape
    modes, groups = residues.shape
    size = width // groups
    steps = rows // SEGS
    tiles = width // LANES
    pitch = FRONT + steps
    part = width // HALVES
    f32 = jnp.float32

    small = [
        pltpu.make_async_copy(a, b, small_sem.at[i])
        for i, (a, b) in enumerate(
            ((decay_rate, params_d), (short_filter, filt), (residues, params_r), (skip_gain, skip))
        )
    ]

    def large(p, half):
        cols = slice(half * part, (half + 1) * part)
        source = (query, key, value)[p].at[:, cols]
        sem = large_sem.at[half if p else HALVES]
        return pltpu.make_async_copy(source, raw.at[p, :, cols], sem)

    def wait_keys_values(half):
        both = raw.at[1:3, :, half * part : (half + 1) * part]
        pltpu.make_async_copy(both, both, large_sem.at[half]).wait()

    small[0].start()
    large(1, 0).start()
    large(2, 0).start()
    small[1].start()
    large(1, 1).start()
    large(2, 1).start()

    me = lax.axis_index("ctx")
    x, z = me // NZ, lax.rem(me, NZ)

    inner = x < NX - 1

    early = z < LATE
    parity = lax.rem(z, 2)
    partner = 1 - 2 * parity

    def takes(half):
        return parity != half

    def sends_to(t):
        ahead = t > z
        if t >= LATE:
            ahead &= z >= RELAY
        return ahead | ((t < z) & inner)

    def hears_from(t):
        heard = (t < z) | ((t > z) & inner)
        return heard & early if t < RELAY else heard

    def sends_half(t, half):
        return sends_to(t) if half != t % 2 else sends_to(t) & (t > z)

    def hears_half(t, half):
        return hears_from(t) & ((t < z) | takes(half))

    barrier = pltpu.get_barrier_semaphore()

    def signal(sem, ctx):
        pl.semaphore_signal(sem, inc=1, device_id={"ctx": ctx}, device_id_type=MESH)

    for t in range(NZ):
        pl.when(hears_from(t))(functools.partial(signal, barrier, x * NZ + t))
    pl.when(early & (x > 0))(functools.partial(signal, barrier, x * NZ - 1))
    for k in range(1, NX):
        pl.when(x + k < NX)(functools.partial(signal, barrier, me + k * NZ))
        pl.when(x + k < NX)(functools.partial(signal, barrier, me + k * NZ + partner))

    for half in range(HALVES):
        large(0, half).start()
    small[2].start()
    small[3].start()

    lane = lax.broadcasted_iota(jnp.int32, (groups, width), 1)
    group = lax.broadcasted_iota(jnp.int32, (groups, width), 0)
    pick = (lane // size == group).astype(f32).astype(jnp.bfloat16)
    pick = jnp.concatenate([pick] * 3, axis=0)

    def per_channel(values):
        high, rest = split_f32(values)
        middle, rest = split_f32(rest)
        parts = jnp.concatenate([high, middle, rest.astype(jnp.bfloat16)], axis=1)
        return jnp.dot(parts, pick, preferred_element_type=f32)

    small[0].wait()
    decay[...] = per_channel(params_d[...])
    row = lax.broadcasted_iota(jnp.int32, (SEGS, LANES), 0)

    def widen(p, t):
        for i in range(SEGS):
            at = i * pitch + FRONT
            wide[p, t, at : at + steps] = raw[
                p, i * steps : (i + 1) * steps, t * LANES : (t + 1) * LANES
            ].astype(f32)
            if i:
                wide[p, t, at - FRONT : at] = wide[p, t, at - pitch + steps - FRONT : at - FRONT]
            else:
                wide[p, t, 0:FRONT] = jnp.zeros((FRONT, LANES), f32)

    def segments(p, offset, tile):
        return wide[p, tile, pl.ds(FRONT + offset, SEGS, stride=pitch)]

    def taps_of(p, cols):
        return [jnp.broadcast_to(filt[p, i : i + 1, cols], (SEGS, LANES)) for i in range(3)]

    def short(taps, now, last, older):
        return taps[0] * now + taps[1] * last + taps[2] * older

    zero = jnp.zeros((SEGS, LANES), f32)

    def pass_a(tile):
        for p in (1, 2):
            if tile == 0 and p == 1:
                wait_keys_values(0)
            widen(p, tile)
        cols = slice(tile * LANES, (tile + 1) * LANES)
        ktaps, vtaps = taps_of(1, cols), taps_of(2, cols)
        rates = [
            jnp.broadcast_to(jnp.exp(-decay[n : n + 1, cols]), (SEGS, LANES)) for n in range(modes)
        ]

        def advance(j, carry):
            k1, k2, v1, v2, states = carry
            k0, v0 = segments(1, j, tile), segments(2, j, tile)
            g = short(ktaps, k0, k1, k2) * short(vtaps, v0, v1, v2)
            gated[pl.ds(pl.multiple_of(j * SEGS, SEGS), SEGS), cols] = g
            states = tuple(s * a + g for s, a in zip(states, rates))
            return k0, k1, v0, v1, states

        first = (
            segments(1, -1, tile), segments(1, -2, tile),
            segments(2, -1, tile), segments(2, -2, tile),
            (zero,) * modes,
        )
        states = lax.fori_loop(0, steps, advance, first, unroll=8)[4]
        for n in range(modes):
            powers = [jnp.exp(-decay[n : n + 1, cols] * (steps * s)) for s in (1, 2, 4)]
            state = scan_segments(states[n], powers, row)
            final[n, :, cols] = state
            half, at = divmod(tile * LANES, part)
            fresh[half, n : n + 1, at : at + LANES] = state[SEGS - 1 : SEGS]

    small[1].wait()
    pass_a(0)
    pass_a(1)

    wait_keys_values(1)
    for half in range(HALVES):
        cols = slice(half * part, (half + 1) * part)
        ends_rows = []
        for p in (1, 2):
            ends_rows.append(raw[p, 0:8, cols].astype(f32)[0:2])
            ends_rows.append(raw[p, rows - 8 : rows, cols].astype(f32)[6:8])
        ends_own[half] = jnp.concatenate(ends_rows, axis=0).astype(jnp.bfloat16)
    last = NX * NZ - 1
    line_count = sum(jnp.where(sends_to(t), 1, 0) for t in range(NZ))
    ends_line_here = (z == NZ - 1) & inner
    pl.semaphore_wait(barrier, line_count + jnp.where(ends_line_here, LATE, 0) + 2 * x)
    for k in range(1, NX):
        pl.when(x >= k)(functools.partial(signal, ready, me - k * NZ))
        pl.when(x >= k)(functools.partial(signal, ready, me - k * NZ + partner))
    rim_copy = to_device(edge, rim, rim_send, rim_recv, me + 1)

    def tail_line(t):
        return to_device(ends_own, ends.at[pl.ds(slot(NZ, 0), HALVES)], tail_send, tail_recv, (x + 1) * NZ + t)

    @pl.when(ends_line_here)
    def _():
        for t in range(LATE):
            tail_line(t).start()

    def group_of(t):
        return jnp.where(z < RELAY, 0, 1) if t == RELAY else 1

    def ends_line(t, half):
        return to_device(
            ends_own.at[half], ends.at[slot(z, half)],
            ends_send, ends_recv.at[group_of(t)], x * NZ + t,
        )

    sooner, later = range(LATE), range(LATE, NZ)
    for half in range(HALVES):
        for t in sooner:
            pl.when(sends_half(t, half))(ends_line(t, half).start)

    def line_copy(t, half):
        return to_device(
            fresh.at[half], lines.at[slot(z, half)],
            line_send, line_recv.at[group_of(t), half], x * NZ + t,
        )

    def send_states(half):
        for t in sooner:
            pl.when(sends_half(t, half))(line_copy(t, half).start)
        lines[slot(z, half)] = fresh[half]

    send_states(0)
    pass_a(2)
    pass_a(3)
    send_states(1)
    for half in range(HALVES):
        ends[slot(z, half)] = ends_own[half]

    small[2].wait()
    weight[...] = per_channel(params_r[...]) * jnp.sqrt(one_minus_exp(2.0 * decay[...]))

    lane = lax.broadcasted_iota(jnp.int32, (modes, width), 1)
    mode = lax.broadcasted_iota(jnp.int32, (modes, width), 0)
    own = lax.rem(lane, modes) == mode
    flat_rate = jnp.sum(jnp.where(own, decay[...], 0.0), axis=0, keepdims=True)
    flat_weight = jnp.sum(jnp.where(own, weight[...], 0.0), axis=0, keepdims=True)
    for tile in range(tiles):
        cols = slice(tile * LANES, (tile + 1) * LANES)
        rate8 = jnp.broadcast_to(flat_rate[:, cols], (16, LANES))
        row16 = lax.broadcasted_iota(jnp.int32, (16, LANES), 0).astype(f32)
        begin = flat_weight[:, cols] * jnp.exp(-rate8 * (row16 + 1.0))
        jump = jnp.exp(-rate8 * 16.0)

        def lead_rows(i, now, cols=cols, jump=jump):
            at = pl.ds(pl.multiple_of(i * 16, 16), 16)
            hi, lo = split(now)
            lead_hi[at, cols] = hi
            lead_lo[at, cols] = lo
            return now * jump

        lax.fori_loop(0, rows // 16, lead_rows, begin, unroll=4)
    tail = [jnp.zeros((2, width), f32)]
    for p in (2, 1, 0):
        if p == 0:
            pltpu.make_async_copy(raw.at[0], raw.at[0], large_sem.at[HALVES]).wait()
        tail.insert(0, raw[p, rows - 8 : rows].astype(f32)[6:8])
    edge[...] = jnp.concatenate(tail, axis=0).astype(jnp.bfloat16)
    pl.when(me < last)(rim_copy.start)
    for t in later:

        for half in range(HALVES):

            @pl.when(sends_half(t, half) & (z >= LATE))
            def _(t=t, half=half):
                ends_line(t, half).start()
                line_copy(t, half).start()

    for tile in range(tiles):
        widen(0, tile)
    small[3].wait()

    def head(p, tile, cols):
        before = rim[:, cols].astype(f32)[2 * p : 2 * p + 2]
        front = jnp.concatenate([before, wide[p, tile, FRONT : FRONT + 2]], axis=0)
        return sum(filt[p, i : i + 1, cols] * front[2 - i : 4 - i] for i in range(3))

    def take_rim():
        @pl.when(me == 0)
        def _():
            rim[...] = jnp.zeros_like(rim)

        pl.when(me > 0)(rim_copy.wait_recv)
        for tile in range(tiles):
            cols = slice(tile * LANES, (tile + 1) * LANES)
            true_head = head(1, tile, cols) * head(2, tile, cols)
            for i in range(2):
                at = slice(i * SEGS, i * SEGS + 1)
                delta_own[i : i + 1, cols] = true_head[i : i + 1] - gated[at, cols]

    def pass_b(tile):
        cols = slice(tile * LANES, (tile + 1) * LANES)
        qtaps = taps_of(0, cols)
        gain = jnp.broadcast_to(skip[0:1, cols], (SEGS, LANES))
        rates, weights, entering = [], [], []
        for n in range(modes):
            entering.append(jnp.where(row >= 1, pltpu.roll(final[n, :, cols], 1, 0), 0.0))
            rates.append(jnp.broadcast_to(jnp.exp(-decay[n : n + 1, cols]), (SEGS, LANES)))
            weights.append(jnp.broadcast_to(weight[n : n + 1, cols], (SEGS, LANES)))

        def respond(j, carry):
            q1, q2, states = carry
            q0 = segments(0, j, tile)
            g = gated[pl.ds(pl.multiple_of(j * SEGS, SEGS), SEGS), cols]
            states = tuple(s * a + g for s, a in zip(states, rates))
            terms = [s * w for s, w in zip(states, weights)] + [gain * g]
            while len(terms) > 1:
                terms = [sum(terms[i : i + 2]) for i in range(0, len(terms), 2)]
            at = pl.ds(j, SEGS, stride=steps)
            base[tile, at] = terms[0]
            qs[tile, at] = short(qtaps, q0, q1, q2)
            return q0, q1, states

        first = (segments(0, -1, tile), segments(0, -2, tile), tuple(entering))
        lax.fori_loop(0, steps, respond, first, unroll=4)

    def corrections(known):
        for t in known:
            for tile in range(tiles):
                half, at = divmod(tile * LANES, part)
                piece = ends[slot(t, half), :, at : at + LANES]
                ends_wide[tile, 8 * t : 8 * t + 8] = piece.astype(f32)
        for tile in range(tiles):
            cols = slice(tile * LANES, (tile + 1) * LANES)
            olds, news = [], []
            for p in (1, 2):
                first, second, before2, before1 = [
                    ends_wide[tile, pl.ds(4 * p - 4 + i, NZ, stride=8)] for i in range(4)
                ]
                line_before = jnp.where(x > 0, ends_wide[tile, 8 * NZ + 4 * p - 2 : 8 * NZ + 4 * p], 0.0)
                before2 = jnp.where(row == 0, line_before[0:1], pltpu.roll(before2, 1, 0))
                before1 = jnp.where(row == 0, line_before[1:2], pltpu.roll(before1, 1, 0))
                now, last1, last2 = [filt[p, i : i + 1, cols] for i in range(3)]
                old0, old1 = now * first, now * second + last1 * first
                olds.append((old0, old1))
                news.append((old0 + last1 * before1 + last2 * before2, old1 + last2 * before1))
            for i in range(2):
                deltas[i, :, cols] = news[0][i] * news[1][i] - olds[0][i] * olds[1][i]

    def own_factors(half):
        rate = decay[:, half * part : (half + 1) * part]
        return jnp.exp(-rate * rows), jnp.exp(-rate * (rows - 1.0)), jnp.exp(-rate * (rows - 2.0))

    def add_line(i, half, carried, block, late0, late1):
        cols = slice(half * part, (half + 1) * part)
        e0, e1 = [deltas[j, i : i + 1, cols] for j in range(2)]
        return carried * block + lines[slot(i, half)] + late0 * e0 + late1 * e1

    def relay_copy(t, half):
        return to_device(
            relayed.at[half], lines.at[slot(RELAY, half)],
            line_send, line_recv.at[1, half], x * NZ + t,
        )

    def relay():
        wait_for(ends_recv.at[0], ends, RELAY * HALVES, RELAY * HALVES)
        for half in range(HALVES):
            wait_for(line_recv.at[0, half], lines, RELAY, RELAY)
        pl.when(x > 0)(tail_line(0).wait_recv)
        corrections([*range(LATE), NZ])
        for half in range(HALVES):
            factors = own_factors(half)
            carried = jnp.zeros((modes, part), f32)
            for i in range(LATE):
                carried = add_line(i, half, carried, *factors)
            relayed[half] = carried
        for t in later:
            for half in range(HALVES):
                ends_line(t, half).start()
                relay_copy(t, half).start()

    pass_b(0)
    pass_b(1)
    pass_b(2)
    pl.when(z == RELAY)(relay)
    pass_b(3)

    pl.when((z < RELAY) & (x > 0))(tail_line(0).wait_recv)
    def heard(half):
        known = jnp.where(z == RELAY, RELAY, 0)
        return count_of(hears_half(t, half) for t in range(NZ)) - known

    wait_for(ends_recv.at[1], ends, heard(0) + heard(1), NZ + 2)
    corrections(range(NZ + 1))
    def total_copy(k, source, half, shift=0):
        return to_device(
            total.at[half], totals.at[slot(source, half)],
            total_send, total_recv.at[half], me + k * NZ + shift,
        )

    def sum_line(half, upto=None):
        factors = own_factors(half)
        carried = jnp.zeros((modes, part), f32)
        for i in range(NZ):
            after = add_line(i, half, carried, *factors)
            if i == RELAY:
                after = jnp.where(early, after, lines[slot(RELAY, half)])
            carried = after if upto is None else jnp.where(upto > i, after, carried)
        return carried

    for half in range(HALVES):
        wait_for(line_recv.at[1, half], lines, heard(half), NZ - 1)

        @pl.when(takes(half) & inner)
        def _(half=half):
            total[half] = sum_line(half)

    pl.when(inner)(lambda: pl.semaphore_wait(ready, 2 * (NX - 1 - x)))
    for half in range(HALVES):
        for k in range(1, NX):
            pl.when((x + k < NX) & takes(half))(total_copy(k, x, half).start)
            pl.when((x + k < NX) & takes(half))(total_copy(k, x, half, partner).start)

    take_rim()
    d0, d1 = delta_own[0:1], delta_own[1:2]
    inverse = jnp.exp(decay[...])
    rim_state = inverse * (d0 + inverse * d1)
    excess = jnp.sum(weight[...] * inverse, axis=0, keepdims=True) * d1
    for tile in range(tiles):
        cols = slice(tile * LANES, (tile + 1) * LANES)
        base[tile, 0:1] += skip[0:1, cols] * d0[:, cols] - excess[:, cols]
        base[tile, 1:2] += skip[0:1, cols] * d1[:, cols]
        qs[tile, 0:2] = head(0, tile, cols)

    for half in range(HALVES):
        own_sum[half] = sum_line(half, z) + rim_state[:, half * part : (half + 1) * part]

    pl.when(me < last)(rim_copy.wait_send)
    sent = count_of(sends_half(t, half) for t in range(NZ) for half in range(HALVES))
    wait_for(ends_send, ends, sent, NZ + RELAY, send=True)
    wait_for(line_send, lines, sent, NZ + RELAY, send=True)
    wait_for(tail_send, ends, jnp.where(ends_line_here, LATE * HALVES, 0), LATE * HALVES, send=True)

    grow = lax.broadcasted_iota(jnp.int32, (part, part), 0) // modes
    gcol = lax.broadcasted_iota(jnp.int32, (part, part), 1) // size
    for half in reversed(range(HALVES)):
        cols = slice(half * part, (half + 1) * part)
        hop = jnp.exp(-decay[:, cols] * (rows * NZ))
        into_line = jnp.exp(-decay[:, cols] * (rows * z.astype(f32)))
        wait_for(total_recv.at[half], totals, x, NX - 1)
        far = jnp.zeros((modes, part), f32)
        for i in range(NX - 1):
            far = jnp.where(x > i, far * hop + totals[slot(i, half)], far)
        state = own_sum[half] + into_line * far
        blocks = jnp.concatenate([state] * (part // modes), axis=0)
        hi, lo = split(jnp.where(grow == gcol, blocks, 0.0))
        lh, ll = lead_hi[:, cols], lead_lo[:, cols]
        add = jnp.dot(lh, hi, preferred_element_type=f32)
        add += jnp.dot(lh, lo, preferred_element_type=f32)
        add += jnp.dot(ll, hi, preferred_element_type=f32)
        for t in range(half * part // LANES, (half + 1) * part // LANES):
            more = add[:, t * LANES - half * part : (t + 1) * LANES - half * part]
            out[:, t * LANES : (t + 1) * LANES] = (qs[t] * (base[t] + more)).astype(jnp.bfloat16)

    wait_for(total_send, totals, 2 * (NX - 1 - x), 2 * (NX - 1), send=True)


def body(query_in, key_in, value_in, residues, decay_rate, short_filter, skip_gain):
    rows, width = query_in.shape
    modes, tiles = residues.shape[0], width // LANES
    pitched = FRONT * SEGS + rows
    half = (modes, width // HALVES)
    f32 = jnp.float32
    vmem = lambda *shape, dtype=f32: pltpu.VMEM(shape, dtype)
    dma = pltpu.SemaphoreType.DMA
    hbm = pl.BlockSpec(memory_space=pltpu.HBM)
    return pl.pallas_call(
        kernel,
        out_shape=jax.ShapeDtypeStruct((rows, width), jnp.bfloat16),
        in_specs=[hbm] * 7,
        out_specs=pl.BlockSpec(memory_space=pltpu.VMEM),
        scratch_shapes=[
            vmem(3, rows, width, dtype=jnp.bfloat16),
            vmem(3, tiles, pitched, LANES),
            vmem(*residues.shape),
            vmem(*decay_rate.shape),
            vmem(*short_filter.shape),
            vmem(*skip_gain.shape),
            vmem(modes, width),
            vmem(modes, width),
            vmem(rows, width),
            vmem(modes, SEGS, width),
            vmem(tiles, rows, LANES),
            vmem(tiles, rows, LANES),
            vmem(rows, width, dtype=jnp.bfloat16),
            vmem(rows, width, dtype=jnp.bfloat16),
            vmem(HALVES, *half),
            vmem(NZ * HALVES, *half),
            vmem(HALVES, *half),
            vmem(8, width, dtype=jnp.bfloat16),
            vmem(8, width, dtype=jnp.bfloat16),
            vmem(HALVES, 8, width // HALVES, dtype=jnp.bfloat16),
            vmem((NZ + 1) * HALVES, 8, width // HALVES, dtype=jnp.bfloat16),
            vmem(tiles, NZ * 8 + 8, LANES),
            vmem(2, NZ, width),
            vmem(2, width),
            vmem(HALVES, *half),
            vmem(NX * HALVES, *half),
            vmem(HALVES, *half),
            dma((4,)), dma((HALVES + 1,)),
            dma, dma((2, HALVES)),
            dma, dma((2,)),
            dma, dma,
            dma, dma((HALVES,)),
            dma, dma,
            pltpu.SemaphoreType.REGULAR,
        ],
        compiler_params=pltpu.CompilerParams(
            collective_id=0, has_side_effects=True, vmem_limit_bytes=40 * 2**20
        ),
    )(
        *(
            pltpu.with_memory_space_constraint(a, pltpu.HBM)
            for a in (query_in, key_in, value_in, residues, decay_rate, short_filter, skip_gain)
        )
    )


def solution(mesh):
    placed = (
        P("ctx", "fsdp"),
        P("ctx", "fsdp"),
        P("ctx", "fsdp"),
        P(None, "fsdp"),
        P(None, "fsdp"),
        P(None, None, "fsdp"),
        P(None, "fsdp"),
    )
    return jax.shard_map(
        body, mesh=mesh, in_specs=placed, out_specs=P("ctx", "fsdp"), check_vma=False
    )
```

```python
import functools

import jax
import jax.numpy as jnp
from jax import lax
from jax.experimental import pallas as pl
from jax.experimental.pallas import tpu as pltpu
from jax.sharding import PartitionSpec as P

MESH = pl.DeviceIdType.MESH
NX, NZ = 4, 8
SEGS = 8
LANES = 128
FRONT = 8
LATE = NZ // 2
RELAY = LATE - 1
HALVES = 2


def to_device(src, dst, send, recv, ctx):
    return pltpu.make_async_remote_copy(
        src_ref=src,
        dst_ref=dst,
        send_sem=send,
        recv_sem=recv,
        device_id={"ctx": ctx},
        device_id_type=MESH,
    )


def wait_for(semaphore, slots, count, most, send=False):
    for n in [count] if isinstance(count, int) else range(1, most + 1):
        some = slots.at[pl.ds(0, n)]
        copy = to_device(some, some, semaphore, semaphore, 0)
        pl.when(count == n)(copy.wait_send if send else copy.wait_recv)


def slot(source, half):
    return source * HALVES + half


def count_of(conditions):
    return sum(jnp.where(condition, 1, 0) for condition in conditions)


def one_minus_exp(u):
    series = u * (1 - u / 2 * (1 - u / 3 * (1 - u / 4 * (1 - u / 5 * (1 - u / 6 * (1 - u / 7))))))
    return jnp.where(u < 0.3, series, 1 - jnp.exp(-u))


def scan_segments(value, powers, row):
    for power, step in zip(powers, (1, 2, 4)):
        value = value + power * jnp.where(row >= step, pltpu.roll(value, step, 0), 0.0)
    return value


def split_f32(x):
    high = x.astype(jnp.bfloat16)
    return high, x - high.astype(jnp.float32)


def split(x):
    high, rest = split_f32(x)
    return high, rest.astype(jnp.bfloat16)


def kernel(
    query, key, value, residues, decay_rate, short_filter, skip_gain,
    out,
    raw, wide, params_r, params_d, filt, skip,
    decay, weight, gated, final, base, qs, lead_hi, lead_lo,
    fresh, lines, relayed, edge, rim, ends_own, ends, ends_wide, deltas, delta_own, total, totals, own_sum,
    small_sem, large_sem, line_send, line_recv, ends_send, ends_recv, tail_send, tail_recv, total_send, total_recv, rim_send, rim_recv,
    ready,
):
    rows, width = query.shape
    modes, groups = residues.shape
    size = width // groups
    steps = rows // SEGS
    tiles = width // LANES
    pitch = FRONT + steps
    part = width // HALVES
    f32 = jnp.float32

    small = [
        pltpu.make_async_copy(a, b, small_sem.at[i])
        for i, (a, b) in enumerate(
            ((decay_rate, params_d), (short_filter, filt), (residues, params_r), (skip_gain, skip))
        )
    ]

    def large(p, half):
        cols = slice(half * part, (half + 1) * part)
        source = (query, key, value)[p].at[:, cols]
        sem = large_sem.at[half if p else HALVES]
        return pltpu.make_async_copy(source, raw.at[p, :, cols], sem)

    def wait_keys_values(half):
        both = raw.at[1:3, :, half * part : (half + 1) * part]
        pltpu.make_async_copy(both, both, large_sem.at[half]).wait()

    small[0].start()
    large(1, 0).start()
    large(2, 0).start()
    small[1].start()
    large(1, 1).start()
    large(2, 1).start()

    me = lax.axis_index("ctx")
    x, z = me // NZ, lax.rem(me, NZ)

    inner = x < NX - 1

    early = z < LATE
    parity = lax.rem(z, 2)
    partner = 1 - 2 * parity

    def takes(half):
        return parity != half

    def sends_to(t):
        ahead = t > z
        if t >= LATE:
            ahead &= z >= RELAY
        return ahead | ((t < z) & inner)

    def hears_from(t):
        heard = (t < z) | ((t > z) & inner)
        return heard & early if t < RELAY else heard

    def sends_half(t, half):
        return sends_to(t) if half != t % 2 else sends_to(t) & (t > z)

    def hears_half(t, half):
        return hears_from(t) & ((t < z) | takes(half))

    barrier = pltpu.get_barrier_semaphore()

    def signal(sem, ctx):
        pl.semaphore_signal(sem, inc=1, device_id={"ctx": ctx}, device_id_type=MESH)

    for t in range(NZ):
        pl.when(hears_from(t))(functools.partial(signal, barrier, x * NZ + t))
    pl.when(early & (x > 0))(functools.partial(signal, barrier, x * NZ - 1))
    for k in range(1, NX):
        pl.when(x + k < NX)(functools.partial(signal, barrier, me + k * NZ))
        pl.when(x + k < NX)(functools.partial(signal, barrier, me + k * NZ + partner))

    for half in range(HALVES):
        large(0, half).start()
    small[2].start()
    small[3].start()

    lane = lax.broadcasted_iota(jnp.int32, (groups, width), 1)
    group = lax.broadcasted_iota(jnp.int32, (groups, width), 0)
    pick = (lane // size == group).astype(f32).astype(jnp.bfloat16)
    pick = jnp.concatenate([pick] * 3, axis=0)

    def per_channel(values):
        high, rest = split_f32(values)
        middle, rest = split_f32(rest)
        parts = jnp.concatenate([high, middle, rest.astype(jnp.bfloat16)], axis=1)
        return jnp.dot(parts, pick, preferred_element_type=f32)

    small[0].wait()
    decay[...] = per_channel(params_d[...])
    row = lax.broadcasted_iota(jnp.int32, (SEGS, LANES), 0)

    def widen(p, t):
        for i in range(SEGS):
            at = i * pitch + FRONT
            wide[p, t, at : at + steps] = raw[
                p, i * steps : (i + 1) * steps, t * LANES : (t + 1) * LANES
            ].astype(f32)
            if i:
                wide[p, t, at - FRONT : at] = wide[p, t, at - pitch + steps - FRONT : at - FRONT]
            else:
                wide[p, t, 0:FRONT] = jnp.zeros((FRONT, LANES), f32)

    def segments(p, offset, tile):
        return wide[p, tile, pl.ds(FRONT + offset, SEGS, stride=pitch)]

    def taps_of(p, cols):
        return [jnp.broadcast_to(filt[p, i : i + 1, cols], (SEGS, LANES)) for i in range(3)]

    def short(taps, now, last, older):
        return taps[0] * now + taps[1] * last + taps[2] * older

    zero = jnp.zeros((SEGS, LANES), f32)

    def pass_a(tile):
        for p in (1, 2):
            if tile == 0 and p == 1:
                wait_keys_values(0)
            widen(p, tile)
        cols = slice(tile * LANES, (tile + 1) * LANES)
        ktaps, vtaps = taps_of(1, cols), taps_of(2, cols)
        rates = [
            jnp.broadcast_to(jnp.exp(-decay[n : n + 1, cols]), (SEGS, LANES)) for n in range(modes)
        ]

        def advance(j, carry):
            k1, k2, v1, v2, states = carry
            k0, v0 = segments(1, j, tile), segments(2, j, tile)
            g = short(ktaps, k0, k1, k2) * short(vtaps, v0, v1, v2)
            gated[pl.ds(pl.multiple_of(j * SEGS, SEGS), SEGS), cols] = g
            states = tuple(s * a + g for s, a in zip(states, rates))
            return k0, k1, v0, v1, states

        first = (
            segments(1, -1, tile), segments(1, -2, tile),
            segments(2, -1, tile), segments(2, -2, tile),
            (zero,) * modes,
        )
        states = lax.fori_loop(0, steps, advance, first, unroll=8)[4]
        for n in range(modes):
            powers = [jnp.exp(-decay[n : n + 1, cols] * (steps * s)) for s in (1, 2, 4)]
            state = scan_segments(states[n], powers, row)
            final[n, :, cols] = state
            half, at = divmod(tile * LANES, part)
            fresh[half, n : n + 1, at : at + LANES] = state[SEGS - 1 : SEGS]

    small[1].wait()
    pass_a(0)
    pass_a(1)

    wait_keys_values(1)
    for half in range(HALVES):
        cols = slice(half * part, (half + 1) * part)
        ends_rows = []
        for p in (1, 2):
            ends_rows.append(raw[p, 0:8, cols].astype(f32)[0:2])
            ends_rows.append(raw[p, rows - 8 : rows, cols].astype(f32)[6:8])
        ends_own[half] = jnp.concatenate(ends_rows, axis=0).astype(jnp.bfloat16)
    last = NX * NZ - 1
    line_count = sum(jnp.where(sends_to(t), 1, 0) for t in range(NZ))
    ends_line_here = (z == NZ - 1) & inner
    pl.semaphore_wait(barrier, line_count + jnp.where(ends_line_here, LATE, 0) + 2 * x)
    for k in range(1, NX):
        pl.when(x >= k)(functools.partial(signal, ready, me - k * NZ))
        pl.when(x >= k)(functools.partial(signal, ready, me - k * NZ + partner))
    rim_copy = to_device(edge, rim, rim_send, rim_recv, me + 1)

    def tail_line(t):
        return to_device(ends_own, ends.at[pl.ds(slot(NZ, 0), HALVES)], tail_send, tail_recv, (x + 1) * NZ + t)

    @pl.when(ends_line_here)
    def _():
        for t in range(LATE):
            tail_line(t).start()

    def group_of(t):
        return jnp.where(z < RELAY, 0, 1) if t == RELAY else 1

    def ends_line(t, half):
        return to_device(
            ends_own.at[half], ends.at[slot(z, half)],
            ends_send, ends_recv.at[group_of(t)], x * NZ + t,
        )

    sooner, later = range(LATE), range(LATE, NZ)
    for half in range(HALVES):
        for t in sooner:
            pl.when(sends_half(t, half))(ends_line(t, half).start)

    def line_copy(t, half):
        return to_device(
            fresh.at[half], lines.at[slot(z, half)],
            line_send, line_recv.at[group_of(t), half], x * NZ + t,
        )

    def send_states(half):
        for t in sooner:
            pl.when(sends_half(t, half))(line_copy(t, half).start)
        lines[slot(z, half)] = fresh[half]

    send_states(0)
    pass_a(2)
    pass_a(3)
    send_states(1)
    for half in range(HALVES):
        ends[slot(z, half)] = ends_own[half]

    small[2].wait()
    weight[...] = per_channel(params_r[...]) * jnp.sqrt(one_minus_exp(2.0 * decay[...]))

    lane = lax.broadcasted_iota(jnp.int32, (modes, width), 1)
    mode = lax.broadcasted_iota(jnp.int32, (modes, width), 0)
    own = lax.rem(lane, modes) == mode
    flat_rate = jnp.sum(jnp.where(own, decay[...], 0.0), axis=0, keepdims=True)
    flat_weight = jnp.sum(jnp.where(own, weight[...], 0.0), axis=0, keepdims=True)
    for tile in range(tiles):
        cols = slice(tile * LANES, (tile + 1) * LANES)
        rate8 = jnp.broadcast_to(flat_rate[:, cols], (16, LANES))
        row16 = lax.broadcasted_iota(jnp.int32, (16, LANES), 0).astype(f32)
        begin = flat_weight[:, cols] * jnp.exp(-rate8 * (row16 + 1.0))
        jump = jnp.exp(-rate8 * 16.0)

        def lead_rows(i, now, cols=cols, jump=jump):
            at = pl.ds(pl.multiple_of(i * 16, 16), 16)
            hi, lo = split(now)
            lead_hi[at, cols] = hi
            lead_lo[at, cols] = lo
            return now * jump

        lax.fori_loop(0, rows // 16, lead_rows, begin, unroll=4)
    tail = [jnp.zeros((2, width), f32)]
    for p in (2, 1, 0):
        if p == 0:
            pltpu.make_async_copy(raw.at[0], raw.at[0], large_sem.at[HALVES]).wait()
        tail.insert(0, raw[p, rows - 8 : rows].astype(f32)[6:8])
    edge[...] = jnp.concatenate(tail, axis=0).astype(jnp.bfloat16)
    pl.when(me < last)(rim_copy.start)
    for t in later:

        for half in range(HALVES):

            @pl.when(sends_half(t, half) & (z >= LATE))
            def _(t=t, half=half):
                ends_line(t, half).start()
                line_copy(t, half).start()

    for tile in range(tiles):
        widen(0, tile)
    small[3].wait()

    def head(p, tile, cols):
        before = rim[:, cols].astype(f32)[2 * p : 2 * p + 2]
        front = jnp.concatenate([before, wide[p, tile, FRONT : FRONT + 2]], axis=0)
        return sum(filt[p, i : i + 1, cols] * front[2 - i : 4 - i] for i in range(3))

    def take_rim():
        @pl.when(me == 0)
        def _():
            rim[...] = jnp.zeros_like(rim)

        pl.when(me > 0)(rim_copy.wait_recv)
        for tile in range(tiles):
            cols = slice(tile * LANES, (tile + 1) * LANES)
            true_head = head(1, tile, cols) * head(2, tile, cols)
            for i in range(2):
                at = slice(i * SEGS, i * SEGS + 1)
                delta_own[i : i + 1, cols] = true_head[i : i + 1] - gated[at, cols]

    def pass_b(tile):
        cols = slice(tile * LANES, (tile + 1) * LANES)
        qtaps = taps_of(0, cols)
        gain = jnp.broadcast_to(skip[0:1, cols], (SEGS, LANES))
        rates, weights, entering = [], [], []
        for n in range(modes):
            entering.append(jnp.where(row >= 1, pltpu.roll(final[n, :, cols], 1, 0), 0.0))
            rates.append(jnp.broadcast_to(jnp.exp(-decay[n : n + 1, cols]), (SEGS, LANES)))
            weights.append(jnp.broadcast_to(weight[n : n + 1, cols], (SEGS, LANES)))

        def respond(j, carry):
            q1, q2, states = carry
            q0 = segments(0, j, tile)
            g = gated[pl.ds(pl.multiple_of(j * SEGS, SEGS), SEGS), cols]
            states = tuple(s * a + g for s, a in zip(states, rates))
            terms = [s * w for s, w in zip(states, weights)] + [gain * g]
            while len(terms) > 1:
                terms = [sum(terms[i : i + 2]) for i in range(0, len(terms), 2)]
            at = pl.ds(j, SEGS, stride=steps)
            base[tile, at] = terms[0]
            qs[tile, at] = short(qtaps, q0, q1, q2)
            return q0, q1, states

        first = (segments(0, -1, tile), segments(0, -2, tile), tuple(entering))
        lax.fori_loop(0, steps, respond, first, unroll=4)

    def corrections(known):
        for t in known:
            for tile in range(tiles):
                half, at = divmod(tile * LANES, part)
                piece = ends[slot(t, half), :, at : at + LANES]
                ends_wide[tile, 8 * t : 8 * t + 8] = piece.astype(f32)
        for tile in range(tiles):
            cols = slice(tile * LANES, (tile + 1) * LANES)
            olds, news = [], []
            for p in (1, 2):
                first, second, before2, before1 = [
                    ends_wide[tile, pl.ds(4 * p - 4 + i, NZ, stride=8)] for i in range(4)
                ]
                line_before = jnp.where(x > 0, ends_wide[tile, 8 * NZ + 4 * p - 2 : 8 * NZ + 4 * p], 0.0)
                before2 = jnp.where(row == 0, line_before[0:1], pltpu.roll(before2, 1, 0))
                before1 = jnp.where(row == 0, line_before[1:2], pltpu.roll(before1, 1, 0))
                now, last1, last2 = [filt[p, i : i + 1, cols] for i in range(3)]
                old0, old1 = now * first, now * second + last1 * first
                olds.append((old0, old1))
                news.append((old0 + last1 * before1 + last2 * before2, old1 + last2 * before1))
            for i in range(2):
                deltas[i, :, cols] = news[0][i] * news[1][i] - olds[0][i] * olds[1][i]

    def own_factors(half):
        rate = decay[:, half * part : (half + 1) * part]
        return jnp.exp(-rate * rows), jnp.exp(-rate * (rows - 1.0)), jnp.exp(-rate * (rows - 2.0))

    def add_line(i, half, carried, block, late0, late1):
        cols = slice(half * part, (half + 1) * part)
        e0, e1 = [deltas[j, i : i + 1, cols] for j in range(2)]
        return carried * block + lines[slot(i, half)] + late0 * e0 + late1 * e1

    def relay_copy(t, half):
        return to_device(
            relayed.at[half], lines.at[slot(RELAY, half)],
            line_send, line_recv.at[1, half], x * NZ + t,
        )

    def relay():
        wait_for(ends_recv.at[0], ends, RELAY * HALVES, RELAY * HALVES)
        for half in range(HALVES):
            wait_for(line_recv.at[0, half], lines, RELAY, RELAY)
        pl.when(x > 0)(tail_line(0).wait_recv)
        corrections([*range(LATE), NZ])
        for half in range(HALVES):
            factors = own_factors(half)
            carried = jnp.zeros((modes, part), f32)
            for i in range(LATE):
                carried = add_line(i, half, carried, *factors)
            relayed[half] = carried
        for t in reversed(later):
            for half in range(HALVES):
                ends_line(t, half).start()
                relay_copy(t, half).start()

    pass_b(0)
    pass_b(1)
    pl.when(z == RELAY)(relay)
    pass_b(2)
    pass_b(3)

    pl.when((z < RELAY) & (x > 0))(tail_line(0).wait_recv)
    def heard(half):
        known = jnp.where(z == RELAY, RELAY, 0)
        return count_of(hears_half(t, half) for t in range(NZ)) - known

    wait_for(ends_recv.at[1], ends, heard(0) + heard(1), NZ + 2)
    corrections(range(NZ + 1))
    def total_copy(k, source, half, shift=0):
        return to_device(
            total.at[half], totals.at[slot(source, half)],
            total_send, total_recv.at[half], me + k * NZ + shift,
        )

    def sum_line(half, upto=None):
        factors = own_factors(half)
        carried = jnp.zeros((modes, part), f32)
        for i in range(NZ):
            after = add_line(i, half, carried, *factors)
            if i == RELAY:
                after = jnp.where(early, after, lines[slot(RELAY, half)])
            carried = after if upto is None else jnp.where(upto > i, after, carried)
        return carried

    for half in range(HALVES):
        wait_for(line_recv.at[1, half], lines, heard(half), NZ - 1)

        @pl.when(takes(half) & inner)
        def _(half=half):
            total[half] = sum_line(half)

    pl.when(inner)(lambda: pl.semaphore_wait(ready, 2 * (NX - 1 - x)))
    for half in range(HALVES):
        for k in range(1, NX):
            pl.when((x + k < NX) & takes(half))(total_copy(k, x, half, -parity).start)
            pl.when((x + k < NX) & takes(half))(total_copy(k, x, half, 1 - parity).start)

    take_rim()
    d0, d1 = delta_own[0:1], delta_own[1:2]
    inverse = jnp.exp(decay[...])
    rim_state = inverse * (d0 + inverse * d1)
    excess = jnp.sum(weight[...] * inverse, axis=0, keepdims=True) * d1
    for tile in range(tiles):
        cols = slice(tile * LANES, (tile + 1) * LANES)
        base[tile, 0:1] += skip[0:1, cols] * d0[:, cols] - excess[:, cols]
        base[tile, 1:2] += skip[0:1, cols] * d1[:, cols]
        qs[tile, 0:2] = head(0, tile, cols)

    for half in range(HALVES):
        own_sum[half] = sum_line(half, z) + rim_state[:, half * part : (half + 1) * part]

    pl.when(me < last)(rim_copy.wait_send)
    sent = count_of(sends_half(t, half) for t in range(NZ) for half in range(HALVES))
    wait_for(ends_send, ends, sent, NZ + RELAY, send=True)
    wait_for(line_send, lines, sent, NZ + RELAY, send=True)
    wait_for(tail_send, ends, jnp.where(ends_line_here, LATE * HALVES, 0), LATE * HALVES, send=True)

    grow = lax.broadcasted_iota(jnp.int32, (part, part), 0) // modes
    gcol = lax.broadcasted_iota(jnp.int32, (part, part), 1) // size
    for half in reversed(range(HALVES)):
        cols = slice(half * part, (half + 1) * part)
        hop = jnp.exp(-decay[:, cols] * (rows * NZ))
        into_line = jnp.exp(-decay[:, cols] * (rows * z.astype(f32)))
        wait_for(total_recv.at[half], totals, x, NX - 1)
        far = jnp.zeros((modes, part), f32)
        for i in range(NX - 1):
            far = jnp.where(x > i, far * hop + totals[slot(i, half)], far)
        state = own_sum[half] + into_line * far
        blocks = jnp.concatenate([state] * (part // modes), axis=0)
        hi, lo = split(jnp.where(grow == gcol, blocks, 0.0))
        lh, ll = lead_hi[:, cols], lead_lo[:, cols]
        add = jnp.dot(lh, hi, preferred_element_type=f32)
        add += jnp.dot(lh, lo, preferred_element_type=f32)
        add += jnp.dot(ll, hi, preferred_element_type=f32)
        for t in range(half * part // LANES, (half + 1) * part // LANES):
            more = add[:, t * LANES - half * part : (t + 1) * LANES - half * part]
            out[:, t * LANES : (t + 1) * LANES] = (qs[t] * (base[t] + more)).astype(jnp.bfloat16)

    wait_for(total_send, totals, 2 * (NX - 1 - x), 2 * (NX - 1), send=True)


def body(query_in, key_in, value_in, residues, decay_rate, short_filter, skip_gain):
    rows, width = query_in.shape
    modes, tiles = residues.shape[0], width // LANES
    pitched = FRONT * SEGS + rows
    half = (modes, width // HALVES)
    f32 = jnp.float32
    vmem = lambda *shape, dtype=f32: pltpu.VMEM(shape, dtype)
    dma = pltpu.SemaphoreType.DMA
    hbm = pl.BlockSpec(memory_space=pltpu.HBM)
    return pl.pallas_call(
        kernel,
        out_shape=jax.ShapeDtypeStruct((rows, width), jnp.bfloat16),
        in_specs=[hbm] * 7,
        out_specs=pl.BlockSpec(memory_space=pltpu.VMEM),
        scratch_shapes=[
            vmem(3, rows, width, dtype=jnp.bfloat16),
            vmem(3, tiles, pitched, LANES),
            vmem(*residues.shape),
            vmem(*decay_rate.shape),
            vmem(*short_filter.shape),
            vmem(*skip_gain.shape),
            vmem(modes, width),
            vmem(modes, width),
            vmem(rows, width),
            vmem(modes, SEGS, width),
            vmem(tiles, rows, LANES),
            vmem(tiles, rows, LANES),
            vmem(rows, width, dtype=jnp.bfloat16),
            vmem(rows, width, dtype=jnp.bfloat16),
            vmem(HALVES, *half),
            vmem(NZ * HALVES, *half),
            vmem(HALVES, *half),
            vmem(8, width, dtype=jnp.bfloat16),
            vmem(8, width, dtype=jnp.bfloat16),
            vmem(HALVES, 8, width // HALVES, dtype=jnp.bfloat16),
            vmem((NZ + 1) * HALVES, 8, width // HALVES, dtype=jnp.bfloat16),
            vmem(tiles, NZ * 8 + 8, LANES),
            vmem(2, NZ, width),
            vmem(2, width),
            vmem(HALVES, *half),
            vmem(NX * HALVES, *half),
            vmem(HALVES, *half),
            dma((4,)), dma((HALVES + 1,)),
            dma, dma((2, HALVES)),
            dma, dma((2,)),
            dma, dma,
            dma, dma((HALVES,)),
            dma, dma,
            pltpu.SemaphoreType.REGULAR,
        ],
        compiler_params=pltpu.CompilerParams(
            collective_id=0, has_side_effects=True, vmem_limit_bytes=40 * 2**20
        ),
    )(
        *(
            pltpu.with_memory_space_constraint(a, pltpu.HBM)
            for a in (query_in, key_in, value_in, residues, decay_rate, short_filter, skip_gain)
        )
    )


def solution(mesh):
    placed = (
        P("ctx", "fsdp"),
        P("ctx", "fsdp"),
        P("ctx", "fsdp"),
        P(None, "fsdp"),
        P(None, "fsdp"),
        P(None, None, "fsdp"),
        P(None, "fsdp"),
    )
    return jax.shard_map(
        body, mesh=mesh, in_specs=placed, out_specs=P("ctx", "fsdp"), check_vma=False
    )
```

```python
import functools

import jax
import jax.numpy as jnp
from jax import lax
from jax.experimental import pallas as pl
from jax.experimental.pallas import tpu as pltpu
from jax.sharding import PartitionSpec as P

MESH = pl.DeviceIdType.MESH
NX, NZ = 4, 8
SEGS = 8
LANES = 128
FRONT = 8
LATE = NZ // 2
RELAY = LATE - 1
HALVES = 2


def to_device(src, dst, send, recv, ctx):
    return pltpu.make_async_remote_copy(
        src_ref=src,
        dst_ref=dst,
        send_sem=send,
        recv_sem=recv,
        device_id={"ctx": ctx},
        device_id_type=MESH,
    )


def wait_for(semaphore, slots, count, most, send=False):
    for n in [count] if isinstance(count, int) else range(1, most + 1):
        some = slots.at[pl.ds(0, n)]
        copy = to_device(some, some, semaphore, semaphore, 0)
        pl.when(count == n)(copy.wait_send if send else copy.wait_recv)


def slot(source, half):
    return source * HALVES + half


def count_of(conditions):
    return sum(jnp.where(condition, 1, 0) for condition in conditions)


def one_minus_exp(u):
    series = u * (1 - u / 2 * (1 - u / 3 * (1 - u / 4 * (1 - u / 5 * (1 - u / 6 * (1 - u / 7))))))
    return jnp.where(u < 0.3, series, 1 - jnp.exp(-u))


def scan_segments(value, powers, row):
    for power, step in zip(powers, (1, 2, 4)):
        value = value + power * jnp.where(row >= step, pltpu.roll(value, step, 0), 0.0)
    return value


def split_f32(x):
    high = x.astype(jnp.bfloat16)
    return high, x - high.astype(jnp.float32)


def split(x):
    high, rest = split_f32(x)
    return high, rest.astype(jnp.bfloat16)


def kernel(
    query, key, value, residues, decay_rate, short_filter, skip_gain,
    out,
    raw, wide, params_r, params_d, filt, skip,
    decay, weight, gated, final, base, qs, lead_hi, lead_lo,
    fresh, lines, relayed, edge, rim, ends_own, ends, ends_wide, deltas, delta_own, total, totals, own_sum,
    small_sem, large_sem, line_send, line_recv, ends_send, ends_recv, tail_send, tail_recv, total_send, total_recv, rim_send, rim_recv,
    ready,
):
    rows, width = query.shape
    modes, groups = residues.shape
    size = width // groups
    steps = rows // SEGS
    tiles = width // LANES
    pitch = FRONT + steps
    part = width // HALVES
    f32 = jnp.float32

    small = [
        pltpu.make_async_copy(a, b, small_sem.at[i])
        for i, (a, b) in enumerate(
            ((decay_rate, params_d), (short_filter, filt), (residues, params_r), (skip_gain, skip))
        )
    ]

    def large(p, half):
        cols = slice(half * part, (half + 1) * part)
        source = (query, key, value)[p].at[:, cols]
        sem = large_sem.at[half if p else HALVES]
        return pltpu.make_async_copy(source, raw.at[p, :, cols], sem)

    def wait_keys_values(half):
        both = raw.at[1:3, :, half * part : (half + 1) * part]
        pltpu.make_async_copy(both, both, large_sem.at[half]).wait()

    small[0].start()
    large(1, 0).start()
    large(2, 0).start()
    small[1].start()
    large(1, 1).start()
    large(2, 1).start()

    me = lax.axis_index("ctx")
    x, z = me // NZ, lax.rem(me, NZ)

    inner = x < NX - 1

    early = z < LATE
    parity = lax.rem(z, 2)
    partner = 1 - 2 * parity

    def takes(half):
        return parity != half

    def sends_to(t):
        ahead = t > z
        if t >= LATE:
            ahead &= z >= RELAY
        return ahead | ((t < z) & inner)

    def hears_from(t):
        heard = (t < z) | ((t > z) & inner)
        return heard & early if t < RELAY else heard

    def sends_half(t, half):
        return sends_to(t) if half != t % 2 else sends_to(t) & (t > z)

    def hears_half(t, half):
        return hears_from(t) & ((t < z) | takes(half))

    barrier = pltpu.get_barrier_semaphore()

    def signal(sem, ctx):
        pl.semaphore_signal(sem, inc=1, device_id={"ctx": ctx}, device_id_type=MESH)

    for t in range(NZ):
        pl.when(hears_from(t))(functools.partial(signal, barrier, x * NZ + t))
    pl.when(early & (x > 0))(functools.partial(signal, barrier, x * NZ - 1))
    for k in range(1, NX):
        pl.when(x + k < NX)(functools.partial(signal, barrier, me + k * NZ))
        pl.when(x + k < NX)(functools.partial(signal, barrier, me + k * NZ + partner))

    for half in range(HALVES):
        large(0, half).start()
    small[2].start()
    small[3].start()

    lane = lax.broadcasted_iota(jnp.int32, (groups, width), 1)
    group = lax.broadcasted_iota(jnp.int32, (groups, width), 0)
    pick = (lane // size == group).astype(f32).astype(jnp.bfloat16)
    pick = jnp.concatenate([pick] * 3, axis=0)

    def per_channel(values):
        high, rest = split_f32(values)
        middle, rest = split_f32(rest)
        parts = jnp.concatenate([high, middle, rest.astype(jnp.bfloat16)], axis=1)
        return jnp.dot(parts, pick, preferred_element_type=f32)

    small[0].wait()
    decay[...] = per_channel(params_d[...])
    row = lax.broadcasted_iota(jnp.int32, (SEGS, LANES), 0)

    def widen_segment(p, t, i):
        cols = slice(t * LANES, (t + 1) * LANES)
        at = pl.multiple_of(i * pitch, FRONT)
        now = raw[p, pl.ds(pl.multiple_of(i * steps, steps), steps), cols].astype(f32)
        wide[p, t, pl.ds(at + FRONT, steps)] = now
        wide[p, t, pl.ds(at + pitch, FRONT)] = now[steps - FRONT :]

    def widen(p, t):
        for i in range(SEGS):
            widen_segment(p, t, i)

    def segments(p, offset, tile):
        return wide[p, tile, pl.ds(FRONT + offset, SEGS, stride=pitch)]

    def taps_of(p, cols):
        return [jnp.broadcast_to(filt[p, i : i + 1, cols], (SEGS, LANES)) for i in range(3)]

    def short(taps, now, last, older):
        return taps[0] * now + taps[1] * last + taps[2] * older

    zero = jnp.zeros((SEGS, LANES), f32)

    def pass_a(tile):
        if tile == 0:
            wait_keys_values(0)
        ahead = tile + 1 < tiles
        if tile == 0:
            widen(1, 0)
            widen(2, 0)
        cols = slice(tile * LANES, (tile + 1) * LANES)
        ktaps, vtaps = taps_of(1, cols), taps_of(2, cols)
        rates = [
            jnp.broadcast_to(jnp.exp(-decay[n : n + 1, cols]), (SEGS, LANES)) for n in range(modes)
        ]

        def advance(i, carry):
            k1, k2, v1, v2, states = carry
            for step in range(SEGS):
                j = i * SEGS + step
                k0, v0 = segments(1, j, tile), segments(2, j, tile)
                g = short(ktaps, k0, k1, k2) * short(vtaps, v0, v1, v2)
                gated[pl.ds(pl.multiple_of(j * SEGS, SEGS), SEGS), cols] = g
                states = tuple(s * a + g for s, a in zip(states, rates))
                k1, k2, v1, v2 = k0, k1, v0, v1
            if ahead:
                widen_segment(1, tile + 1, i)
                widen_segment(2, tile + 1, i)
            return k1, k2, v1, v2, states

        first = (
            segments(1, -1, tile), segments(1, -2, tile),
            segments(2, -1, tile), segments(2, -2, tile),
            (zero,) * modes,
        )
        states = lax.fori_loop(0, steps // SEGS, advance, first)[4]
        for n in range(modes):
            powers = [jnp.exp(-decay[n : n + 1, cols] * (steps * s)) for s in (1, 2, 4)]
            state = scan_segments(states[n], powers, row)
            final[n, :, cols] = state
            half, at = divmod(tile * LANES, part)
            fresh[half, n : n + 1, at : at + LANES] = state[SEGS - 1 : SEGS]

    for p in range(3):
        for t in range(tiles):
            wide[p, t, 0:FRONT] = jnp.zeros((FRONT, LANES), f32)
    small[1].wait()
    pass_a(0)
    wait_keys_values(1)
    pass_a(1)

    for half in range(HALVES):
        cols = slice(half * part, (half + 1) * part)
        ends_rows = []
        for p in (1, 2):
            ends_rows.append(raw[p, 0:8, cols].astype(f32)[0:2])
            ends_rows.append(raw[p, rows - 8 : rows, cols].astype(f32)[6:8])
        ends_own[half] = jnp.concatenate(ends_rows, axis=0).astype(jnp.bfloat16)
    last = NX * NZ - 1
    line_count = sum(jnp.where(sends_to(t), 1, 0) for t in range(NZ))
    ends_line_here = (z == NZ - 1) & inner
    pl.semaphore_wait(barrier, line_count + jnp.where(ends_line_here, LATE, 0) + 2 * x)
    rim_copy = to_device(edge, rim, rim_send, rim_recv, me + 1)

    def tail_line(t):
        return to_device(ends_own, ends.at[pl.ds(slot(NZ, 0), HALVES)], tail_send, tail_recv, (x + 1) * NZ + t)

    @pl.when(ends_line_here)
    def _():
        for t in range(LATE):
            tail_line(t).start()

    def group_of(t):
        return jnp.where(z < RELAY, 0, 1) if t == RELAY else 1

    def ends_line(t, half):
        return to_device(
            ends_own.at[half], ends.at[slot(z, half)],
            ends_send, ends_recv.at[group_of(t)], x * NZ + t,
        )

    sooner, later = range(LATE), range(LATE, NZ)
    for half in range(HALVES):
        for t in sooner:
            pl.when(sends_half(t, half))(ends_line(t, half).start)

    def line_copy(t, half):
        return to_device(
            fresh.at[half], lines.at[slot(z, half)],
            line_send, line_recv.at[group_of(t), half], x * NZ + t,
        )

    def send_states(half):
        for t in sooner:
            pl.when(sends_half(t, half))(line_copy(t, half).start)
        lines[slot(z, half)] = fresh[half]

    send_states(0)
    pass_a(2)
    pass_a(3)
    send_states(1)
    for k in range(1, NX):
        pl.when(x >= k)(functools.partial(signal, ready, me - k * NZ))
        pl.when(x >= k)(functools.partial(signal, ready, me - k * NZ + partner))
    for half in range(HALVES):
        ends[slot(z, half)] = ends_own[half]

    small[2].wait()
    weight[...] = per_channel(params_r[...]) * jnp.sqrt(one_minus_exp(2.0 * decay[...]))

    lane = lax.broadcasted_iota(jnp.int32, (modes, width), 1)
    mode = lax.broadcasted_iota(jnp.int32, (modes, width), 0)
    own = lax.rem(lane, modes) == mode
    flat_rate = jnp.sum(jnp.where(own, decay[...], 0.0), axis=0, keepdims=True)
    flat_weight = jnp.sum(jnp.where(own, weight[...], 0.0), axis=0, keepdims=True)
    for tile in range(tiles):
        cols = slice(tile * LANES, (tile + 1) * LANES)
        rate8 = jnp.broadcast_to(flat_rate[:, cols], (16, LANES))
        row16 = lax.broadcasted_iota(jnp.int32, (16, LANES), 0).astype(f32)
        begin = flat_weight[:, cols] * jnp.exp(-rate8 * (row16 + 1.0))
        jump = jnp.exp(-rate8 * 16.0)

        def lead_rows(i, now, cols=cols, jump=jump):
            at = pl.ds(pl.multiple_of(i * 16, 16), 16)
            hi, lo = split(now)
            lead_hi[at, cols] = hi
            lead_lo[at, cols] = lo
            return now * jump

        lax.fori_loop(0, rows // 16, lead_rows, begin, unroll=4)
    tail = [jnp.zeros((2, width), f32)]
    for p in (2, 1, 0):
        if p == 0:
            pltpu.make_async_copy(raw.at[0], raw.at[0], large_sem.at[HALVES]).wait()
        tail.insert(0, raw[p, rows - 8 : rows].astype(f32)[6:8])
    edge[...] = jnp.concatenate(tail, axis=0).astype(jnp.bfloat16)
    pl.when(me < last)(rim_copy.start)
    for t in later:

        for half in range(HALVES):

            @pl.when(sends_half(t, half) & (z >= LATE))
            def _(t=t, half=half):
                ends_line(t, half).start()
                line_copy(t, half).start()

    for tile in range(tiles):
        widen(0, tile)
    small[3].wait()

    def head(p, tile, cols):
        before = rim[:, cols].astype(f32)[2 * p : 2 * p + 2]
        front = jnp.concatenate([before, wide[p, tile, FRONT : FRONT + 2]], axis=0)
        return sum(filt[p, i : i + 1, cols] * front[2 - i : 4 - i] for i in range(3))

    def take_rim():
        @pl.when(me == 0)
        def _():
            rim[...] = jnp.zeros_like(rim)

        pl.when(me > 0)(rim_copy.wait_recv)
        for tile in range(tiles):
            cols = slice(tile * LANES, (tile + 1) * LANES)
            true_head = head(1, tile, cols) * head(2, tile, cols)
            for i in range(2):
                at = slice(i * SEGS, i * SEGS + 1)
                delta_own[i : i + 1, cols] = true_head[i : i + 1] - gated[at, cols]

    def pass_b(tile):
        cols = slice(tile * LANES, (tile + 1) * LANES)
        qtaps = taps_of(0, cols)
        gain = jnp.broadcast_to(skip[0:1, cols], (SEGS, LANES))
        rates, weights, entering = [], [], []
        for n in range(modes):
            entering.append(jnp.where(row >= 1, pltpu.roll(final[n, :, cols], 1, 0), 0.0))
            rates.append(jnp.broadcast_to(jnp.exp(-decay[n : n + 1, cols]), (SEGS, LANES)))
            weights.append(jnp.broadcast_to(weight[n : n + 1, cols], (SEGS, LANES)))

        def respond(j, carry):
            q1, q2, states = carry
            q0 = segments(0, j, tile)
            g = gated[pl.ds(pl.multiple_of(j * SEGS, SEGS), SEGS), cols]
            states = tuple(s * a + g for s, a in zip(states, rates))
            terms = [s * w for s, w in zip(states, weights)] + [gain * g]
            while len(terms) > 1:
                terms = [sum(terms[i : i + 2]) for i in range(0, len(terms), 2)]
            at = pl.ds(j, SEGS, stride=steps)
            base[tile, at] = terms[0]
            qs[tile, at] = short(qtaps, q0, q1, q2)
            return q0, q1, states

        first = (segments(0, -1, tile), segments(0, -2, tile), tuple(entering))
        lax.fori_loop(0, steps, respond, first, unroll=4)

    def corrections(known):
        for t in known:
            for tile in range(tiles):
                half, at = divmod(tile * LANES, part)
                piece = ends[slot(t, half), :, at : at + LANES]
                ends_wide[tile, 8 * t : 8 * t + 8] = piece.astype(f32)
        for tile in range(tiles):
            cols = slice(tile * LANES, (tile + 1) * LANES)
            olds, news = [], []
            for p in (1, 2):
                first, second, before2, before1 = [
                    ends_wide[tile, pl.ds(4 * p - 4 + i, NZ, stride=8)] for i in range(4)
                ]
                line_before = jnp.where(x > 0, ends_wide[tile, 8 * NZ + 4 * p - 2 : 8 * NZ + 4 * p], 0.0)
                before2 = jnp.where(row == 0, line_before[0:1], pltpu.roll(before2, 1, 0))
                before1 = jnp.where(row == 0, line_before[1:2], pltpu.roll(before1, 1, 0))
                now, last1, last2 = [filt[p, i : i + 1, cols] for i in range(3)]
                old0, old1 = now * first, now * second + last1 * first
                olds.append((old0, old1))
                news.append((old0 + last1 * before1 + last2 * before2, old1 + last2 * before1))
            for i in range(2):
                deltas[i, :, cols] = news[0][i] * news[1][i] - olds[0][i] * olds[1][i]

    def own_factors(half):
        rate = decay[:, half * part : (half + 1) * part]
        return jnp.exp(-rate * rows), jnp.exp(-rate * (rows - 1.0)), jnp.exp(-rate * (rows - 2.0))

    def add_line(i, half, carried, block, late0, late1):
        cols = slice(half * part, (half + 1) * part)
        e0, e1 = [deltas[j, i : i + 1, cols] for j in range(2)]
        return carried * block + lines[slot(i, half)] + late0 * e0 + late1 * e1

    def relay_copy(t, half):
        return to_device(
            relayed.at[half], lines.at[slot(RELAY, half)],
            line_send, line_recv.at[1, half], x * NZ + t,
        )

    def relay():
        wait_for(ends_recv.at[0], ends, RELAY * HALVES, RELAY * HALVES)
        for half in range(HALVES):
            wait_for(line_recv.at[0, half], lines, RELAY, RELAY)
        pl.when(x > 0)(tail_line(0).wait_recv)
        corrections([*range(LATE), NZ])
        for half in range(HALVES):
            factors = own_factors(half)
            carried = jnp.zeros((modes, part), f32)
            for i in range(LATE):
                carried = add_line(i, half, carried, *factors)
            relayed[half] = carried
        for t in reversed(later):
            for half in range(HALVES):
                ends_line(t, half).start()
                relay_copy(t, half).start()

    pass_b(0)
    pass_b(1)
    pl.when(z == RELAY)(relay)
    pass_b(2)
    pass_b(3)

    pl.when((z < RELAY) & (x > 0))(tail_line(0).wait_recv)
    def heard(half):
        known = jnp.where(z == RELAY, RELAY, 0)
        return count_of(hears_half(t, half) for t in range(NZ)) - known

    wait_for(ends_recv.at[1], ends, heard(0) + heard(1), NZ + 2)
    corrections(range(NZ + 1))
    def total_copy(k, source, half, shift=0):
        return to_device(
            total.at[half], totals.at[slot(source, half)],
            total_send, total_recv.at[half], me + k * NZ + shift,
        )

    def sum_line(half, upto=None):
        factors = own_factors(half)
        carried = jnp.zeros((modes, part), f32)
        for i in range(NZ):
            after = add_line(i, half, carried, *factors)
            if i == RELAY:
                after = jnp.where(early, after, lines[slot(RELAY, half)])
            carried = after if upto is None else jnp.where(upto > i, after, carried)
        return carried

    for half in range(HALVES):
        wait_for(line_recv.at[1, half], lines, heard(half), NZ - 1)

        @pl.when(takes(half) & inner)
        def _(half=half):
            total[half] = sum_line(half)

    pl.when(inner)(lambda: pl.semaphore_wait(ready, 2 * (NX - 1 - x)))
    for half in reversed(range(HALVES)):
        for k in range(1, NX):
            pl.when((x + k < NX) & takes(half))(total_copy(k, x, half, -parity).start)
            pl.when((x + k < NX) & takes(half))(total_copy(k, x, half, 1 - parity).start)

    take_rim()
    d0, d1 = delta_own[0:1], delta_own[1:2]
    inverse = jnp.exp(decay[...])
    rim_state = inverse * (d0 + inverse * d1)
    excess = jnp.sum(weight[...] * inverse, axis=0, keepdims=True) * d1
    for tile in range(tiles):
        cols = slice(tile * LANES, (tile + 1) * LANES)
        base[tile, 0:1] += skip[0:1, cols] * d0[:, cols] - excess[:, cols]
        base[tile, 1:2] += skip[0:1, cols] * d1[:, cols]
        qs[tile, 0:2] = head(0, tile, cols)

    for half in range(HALVES):
        own_sum[half] = sum_line(half, z) + rim_state[:, half * part : (half + 1) * part]

    pl.when(me < last)(rim_copy.wait_send)
    sent = count_of(sends_half(t, half) for t in range(NZ) for half in range(HALVES))
    wait_for(ends_send, ends, sent, NZ + RELAY, send=True)
    wait_for(line_send, lines, sent, NZ + RELAY, send=True)
    wait_for(tail_send, ends, jnp.where(ends_line_here, LATE * HALVES, 0), LATE * HALVES, send=True)

    grow = lax.broadcasted_iota(jnp.int32, (part, part), 0) // modes
    gcol = lax.broadcasted_iota(jnp.int32, (part, part), 1) // size
    for half in reversed(range(HALVES)):
        cols = slice(half * part, (half + 1) * part)
        hop = jnp.exp(-decay[:, cols] * (rows * NZ))
        into_line = jnp.exp(-decay[:, cols] * (rows * z.astype(f32)))
        wait_for(total_recv.at[half], totals, x, NX - 1)
        far = jnp.zeros((modes, part), f32)
        for i in range(NX - 1):
            far = jnp.where(x > i, far * hop + totals[slot(i, half)], far)
        state = own_sum[half] + into_line * far
        blocks = jnp.concatenate([state] * (part // modes), axis=0)
        hi, lo = split(jnp.where(grow == gcol, blocks, 0.0))
        for piece in range(2):
            at = slice(piece * rows // 2, (piece + 1) * rows // 2)
            lh, ll = lead_hi[at, cols], lead_lo[at, cols]
            add = jnp.dot(lh, hi, preferred_element_type=f32)
            add += jnp.dot(lh, lo, preferred_element_type=f32)
            add += jnp.dot(ll, hi, preferred_element_type=f32)
            for t in range(half * part // LANES, (half + 1) * part // LANES):
                more = add[:, t * LANES - half * part : (t + 1) * LANES - half * part]
                out[at, t * LANES : (t + 1) * LANES] = (
                    qs[t, at] * (base[t, at] + more)
                ).astype(jnp.bfloat16)

    wait_for(total_send, totals, 2 * (NX - 1 - x), 2 * (NX - 1), send=True)


def body(query_in, key_in, value_in, residues, decay_rate, short_filter, skip_gain):
    rows, width = query_in.shape
    modes, tiles = residues.shape[0], width // LANES
    pitched = FRONT * SEGS + rows
    half = (modes, width // HALVES)
    f32 = jnp.float32
    vmem = lambda *shape, dtype=f32: pltpu.VMEM(shape, dtype)
    dma = pltpu.SemaphoreType.DMA
    hbm = pl.BlockSpec(memory_space=pltpu.HBM)
    return pl.pallas_call(
        kernel,
        out_shape=jax.ShapeDtypeStruct((rows, width), jnp.bfloat16),
        in_specs=[hbm] * 7,
        out_specs=pl.BlockSpec(memory_space=pltpu.VMEM),
        scratch_shapes=[
            vmem(3, rows, width, dtype=jnp.bfloat16),
            vmem(3, tiles, pitched + FRONT, LANES),
            vmem(*residues.shape),
            vmem(*decay_rate.shape),
            vmem(*short_filter.shape),
            vmem(*skip_gain.shape),
            vmem(modes, width),
            vmem(modes, width),
            vmem(rows, width),
            vmem(modes, SEGS, width),
            vmem(tiles, rows, LANES),
            vmem(tiles, rows, LANES),
            vmem(rows, width, dtype=jnp.bfloat16),
            vmem(rows, width, dtype=jnp.bfloat16),
            vmem(HALVES, *half),
            vmem(NZ * HALVES, *half),
            vmem(HALVES, *half),
            vmem(8, width, dtype=jnp.bfloat16),
            vmem(8, width, dtype=jnp.bfloat16),
            vmem(HALVES, 8, width // HALVES, dtype=jnp.bfloat16),
            vmem((NZ + 1) * HALVES, 8, width // HALVES, dtype=jnp.bfloat16),
            vmem(tiles, NZ * 8 + 8, LANES),
            vmem(2, NZ, width),
            vmem(2, width),
            vmem(HALVES, *half),
            vmem(NX * HALVES, *half),
            vmem(HALVES, *half),
            dma((4,)), dma((HALVES + 1,)),
            dma, dma((2, HALVES)),
            dma, dma((2,)),
            dma, dma,
            dma, dma((HALVES,)),
            dma, dma,
            pltpu.SemaphoreType.REGULAR,
        ],
        compiler_params=pltpu.CompilerParams(
            collective_id=0, has_side_effects=True, vmem_limit_bytes=40 * 2**20
        ),
    )(
        *(
            pltpu.with_memory_space_constraint(a, pltpu.HBM)
            for a in (query_in, key_in, value_in, residues, decay_rate, short_filter, skip_gain)
        )
    )


def solution(mesh):
    placed = (
        P("ctx", "fsdp"),
        P("ctx", "fsdp"),
        P("ctx", "fsdp"),
        P(None, "fsdp"),
        P(None, "fsdp"),
        P(None, None, "fsdp"),
        P(None, "fsdp"),
    )
    return jax.shard_map(
        body, mesh=mesh, in_specs=placed, out_specs=P("ctx", "fsdp"), check_vma=False
    )
```

```python
import functools

import jax
import jax.numpy as jnp
from jax import lax
from jax.experimental import pallas as pl
from jax.experimental.pallas import tpu as pltpu
from jax.sharding import PartitionSpec as P

MESH = pl.DeviceIdType.MESH
NX, NZ = 4, 8
SEGS = 8
LANES = 128
FRONT = 8
LATE = NZ // 2
RELAY = LATE - 1
HALVES = 2


def to_device(src, dst, send, recv, ctx):
    return pltpu.make_async_remote_copy(
        src_ref=src,
        dst_ref=dst,
        send_sem=send,
        recv_sem=recv,
        device_id={"ctx": ctx},
        device_id_type=MESH,
    )


def wait_for(semaphore, slots, count, most, send=False):
    for n in [count] if isinstance(count, int) else range(1, most + 1):
        some = slots.at[pl.ds(0, n)]
        copy = to_device(some, some, semaphore, semaphore, 0)
        pl.when(count == n)(copy.wait_send if send else copy.wait_recv)


def slot(source, half):
    return source * HALVES + half


def count_of(conditions):
    return sum(jnp.where(condition, 1, 0) for condition in conditions)


def one_minus_exp(u):
    series = u * (1 - u / 2 * (1 - u / 3 * (1 - u / 4 * (1 - u / 5 * (1 - u / 6 * (1 - u / 7))))))
    return jnp.where(u < 0.3, series, 1 - jnp.exp(-u))


def scan_segments(value, powers, row):
    for power, step in zip(powers, (1, 2, 4)):
        value = value + power * jnp.where(row >= step, pltpu.roll(value, step, 0), 0.0)
    return value


def split_f32(x):
    high = x.astype(jnp.bfloat16)
    return high, x - high.astype(jnp.float32)


def split(x):
    high, rest = split_f32(x)
    return high, rest.astype(jnp.bfloat16)


def kernel(
    query, key, value, residues, decay_rate, short_filter, skip_gain,
    out,
    raw, wide, params_r, params_d, filt, skip,
    decay, weight, gated, final, base, qs, lead_hi, lead_lo,
    fresh, lines, relayed, edge, rim, ends_own, ends, ends_wide, deltas, delta_own, total, totals, own_sum,
    small_sem, large_sem, line_send, line_recv, ends_send, ends_recv, tail_send, tail_recv, total_send, total_recv, rim_send, rim_recv,
    ready,
):
    rows, width = query.shape
    modes, groups = residues.shape
    size = width // groups
    steps = rows // SEGS
    tiles = width // LANES
    pitch = FRONT + steps
    part = width // HALVES
    f32 = jnp.float32

    small = [
        pltpu.make_async_copy(a, b, small_sem.at[i])
        for i, (a, b) in enumerate(
            ((decay_rate, params_d), (short_filter, filt), (residues, params_r), (skip_gain, skip))
        )
    ]

    def large(p, half):
        cols = slice(half * part, (half + 1) * part)
        source = (query, key, value)[p].at[:, cols]
        sem = large_sem.at[half if p else HALVES]
        return pltpu.make_async_copy(source, raw.at[p, :, cols], sem)

    def wait_keys_values(half):
        both = raw.at[1:3, :, half * part : (half + 1) * part]
        pltpu.make_async_copy(both, both, large_sem.at[half]).wait()

    small[0].start()
    small[1].start()
    large(1, 0).start()
    large(2, 0).start()
    large(1, 1).start()
    large(2, 1).start()

    me = lax.axis_index("ctx")
    x, z = me // NZ, lax.rem(me, NZ)

    inner = x < NX - 1

    early = z < LATE
    parity = lax.rem(z, 2)
    partner = 1 - 2 * parity

    def takes(half):
        return parity != half

    def sends_to(t):
        ahead = t > z
        if t >= LATE:
            ahead &= z >= RELAY
        return ahead | ((t < z) & inner)

    def hears_from(t):
        heard = (t < z) | ((t > z) & inner)
        return heard & early if t < RELAY else heard

    def sends_half(t, half):
        return sends_to(t) if half != t % 2 else sends_to(t) & (t > z)

    def hears_half(t, half):
        return hears_from(t) & ((t < z) | takes(half))

    barrier = pltpu.get_barrier_semaphore()

    def signal(sem, ctx):
        pl.semaphore_signal(sem, inc=1, device_id={"ctx": ctx}, device_id_type=MESH)

    for t in range(NZ):
        pl.when(hears_from(t))(functools.partial(signal, barrier, x * NZ + t))
    pl.when(early & (x > 0))(functools.partial(signal, barrier, x * NZ - 1))
    for k in range(1, NX):
        pl.when(x + k < NX)(functools.partial(signal, barrier, me + k * NZ))
        pl.when(x + k < NX)(functools.partial(signal, barrier, me + k * NZ + partner))

    for half in range(HALVES):
        large(0, half).start()
    small[2].start()
    small[3].start()

    lane = lax.broadcasted_iota(jnp.int32, (groups, width), 1)
    group = lax.broadcasted_iota(jnp.int32, (groups, width), 0)
    pick = (lane // size == group).astype(f32).astype(jnp.bfloat16)
    pick = jnp.concatenate([pick] * 3, axis=0)

    def per_channel(values):
        high, rest = split_f32(values)
        middle, rest = split_f32(rest)
        parts = jnp.concatenate([high, middle, rest.astype(jnp.bfloat16)], axis=1)
        return jnp.dot(parts, pick, preferred_element_type=f32)

    small[0].wait()
    decay[...] = per_channel(params_d[...])
    row = lax.broadcasted_iota(jnp.int32, (SEGS, LANES), 0)

    def widen_segment(p, t, i):
        cols = slice(t * LANES, (t + 1) * LANES)
        at = pl.multiple_of(i * pitch, FRONT)
        now = raw[p, pl.ds(pl.multiple_of(i * steps, steps), steps), cols].astype(f32)
        wide[p, t, pl.ds(at + FRONT, steps)] = now
        wide[p, t, pl.ds(at + pitch, FRONT)] = now[steps - FRONT :]

    def widen(p, t):
        for i in range(SEGS):
            widen_segment(p, t, i)

    def segments(p, offset, tile):
        return wide[p, tile, pl.ds(FRONT + offset, SEGS, stride=pitch)]

    def taps_of(p, cols):
        return [jnp.broadcast_to(filt[p, i : i + 1, cols], (SEGS, LANES)) for i in range(3)]

    def short(taps, now, last, older):
        return taps[0] * now + taps[1] * last + taps[2] * older

    zero = jnp.zeros((SEGS, LANES), f32)

    def pass_a(tile):
        if tile == 0:
            wait_keys_values(0)
        ahead = tile + 1 < tiles
        if tile == 0:
            widen(1, 0)
            widen(2, 0)
        cols = slice(tile * LANES, (tile + 1) * LANES)
        ktaps, vtaps = taps_of(1, cols), taps_of(2, cols)
        rates = [
            jnp.broadcast_to(jnp.exp(-decay[n : n + 1, cols]), (SEGS, LANES)) for n in range(modes)
        ]

        def advance(i, carry):
            k1, k2, v1, v2, states = carry
            for step in range(SEGS):
                j = i * SEGS + step
                k0, v0 = segments(1, j, tile), segments(2, j, tile)
                g = short(ktaps, k0, k1, k2) * short(vtaps, v0, v1, v2)
                gated[pl.ds(pl.multiple_of(j * SEGS, SEGS), SEGS), cols] = g
                states = tuple(s * a + g for s, a in zip(states, rates))
                k1, k2, v1, v2 = k0, k1, v0, v1
            if ahead:
                widen_segment(1, tile + 1, i)
                widen_segment(2, tile + 1, i)
            return k1, k2, v1, v2, states

        first = (
            segments(1, -1, tile), segments(1, -2, tile),
            segments(2, -1, tile), segments(2, -2, tile),
            (zero,) * modes,
        )
        states = lax.fori_loop(0, steps // SEGS, advance, first)[4]
        for n in range(modes):
            powers = [jnp.exp(-decay[n : n + 1, cols] * (steps * s)) for s in (1, 2, 4)]
            state = scan_segments(states[n], powers, row)
            final[n, :, cols] = state
            half, at = divmod(tile * LANES, part)
            fresh[half, n : n + 1, at : at + LANES] = state[SEGS - 1 : SEGS]

    for p in range(3):
        for t in range(tiles):
            wide[p, t, 0:FRONT] = jnp.zeros((FRONT, LANES), f32)
    small[1].wait()
    pass_a(0)
    wait_keys_values(1)
    pass_a(1)

    last = NX * NZ - 1
    line_count = sum(jnp.where(sends_to(t), 1, 0) for t in range(NZ))
    ends_line_here = (z == NZ - 1) & inner
    pl.semaphore_wait(barrier, line_count + jnp.where(ends_line_here, LATE, 0) + 2 * x)
    rim_copy = to_device(edge, rim, rim_send, rim_recv, me + 1)

    def tail_line(t):
        return to_device(ends_own, ends.at[pl.ds(slot(NZ, 0), HALVES)], tail_send, tail_recv, (x + 1) * NZ + t)

    def group_of(t):
        return jnp.where(z < RELAY, 0, 1) if t == RELAY else 1

    def ends_line(t, half):
        return to_device(
            ends_own.at[half], ends.at[slot(z, half)],
            ends_send, ends_recv.at[group_of(t)], x * NZ + t,
        )

    sooner, later = range(LATE), range(LATE, NZ)
    def line_copy(t, half):
        return to_device(
            fresh.at[half], lines.at[slot(z, half)],
            line_send, line_recv.at[group_of(t), half], x * NZ + t,
        )

    def send_states(half):
        for t in sooner:
            pl.when(sends_half(t, half))(line_copy(t, half).start)
        lines[slot(z, half)] = fresh[half]

    send_states(0)

    for half in range(HALVES):
        cols = slice(half * part, (half + 1) * part)
        ends_rows = []
        for p in (1, 2):
            ends_rows.append(raw[p, 0:8, cols].astype(f32)[0:2])
            ends_rows.append(raw[p, rows - 8 : rows, cols].astype(f32)[6:8])
        ends_own[half] = jnp.concatenate(ends_rows, axis=0).astype(jnp.bfloat16)

    @pl.when(ends_line_here)
    def _():
        for t in range(LATE):
            tail_line(t).start()

    for half in range(HALVES):
        for t in sooner:
            pl.when(sends_half(t, half))(ends_line(t, half).start)

    pass_a(2)
    pass_a(3)
    send_states(1)
    for k in range(1, NX):
        pl.when(x >= k)(functools.partial(signal, ready, me - k * NZ))
        pl.when(x >= k)(functools.partial(signal, ready, me - k * NZ + partner))
    for half in range(HALVES):
        ends[slot(z, half)] = ends_own[half]

    small[2].wait()
    weight[...] = per_channel(params_r[...]) * jnp.sqrt(one_minus_exp(2.0 * decay[...]))

    lane = lax.broadcasted_iota(jnp.int32, (modes, width), 1)
    mode = lax.broadcasted_iota(jnp.int32, (modes, width), 0)
    own = lax.rem(lane, modes) == mode
    flat_rate = jnp.sum(jnp.where(own, decay[...], 0.0), axis=0, keepdims=True)
    flat_weight = jnp.sum(jnp.where(own, weight[...], 0.0), axis=0, keepdims=True)
    for tile in range(tiles):
        cols = slice(tile * LANES, (tile + 1) * LANES)
        rate8 = jnp.broadcast_to(flat_rate[:, cols], (16, LANES))
        row16 = lax.broadcasted_iota(jnp.int32, (16, LANES), 0).astype(f32)
        begin = flat_weight[:, cols] * jnp.exp(-rate8 * (row16 + 1.0))
        jump = jnp.exp(-rate8 * 16.0)

        def lead_rows(i, now, cols=cols, jump=jump):
            at = pl.ds(pl.multiple_of(i * 16, 16), 16)
            hi, lo = split(now)
            lead_hi[at, cols] = hi
            lead_lo[at, cols] = lo
            return now * jump

        lax.fori_loop(0, rows // 16, lead_rows, begin, unroll=4)
    tail = [jnp.zeros((2, width), f32)]
    for p in (2, 1, 0):
        if p == 0:
            pltpu.make_async_copy(raw.at[0], raw.at[0], large_sem.at[HALVES]).wait()
        tail.insert(0, raw[p, rows - 8 : rows].astype(f32)[6:8])
    edge[...] = jnp.concatenate(tail, axis=0).astype(jnp.bfloat16)
    pl.when(me < last)(rim_copy.start)
    for t in later:

        for half in range(HALVES):

            @pl.when(sends_half(t, half) & (z >= LATE))
            def _(t=t, half=half):
                ends_line(t, half).start()
                line_copy(t, half).start()

    for tile in range(tiles):
        widen(0, tile)
    small[3].wait()

    def head(p, tile, cols):
        before = rim[:, cols].astype(f32)[2 * p : 2 * p + 2]
        front = jnp.concatenate([before, wide[p, tile, FRONT : FRONT + 2]], axis=0)
        return sum(filt[p, i : i + 1, cols] * front[2 - i : 4 - i] for i in range(3))

    def take_rim():
        @pl.when(me == 0)
        def _():
            rim[...] = jnp.zeros_like(rim)

        pl.when(me > 0)(rim_copy.wait_recv)
        for tile in range(tiles):
            cols = slice(tile * LANES, (tile + 1) * LANES)
            true_head = head(1, tile, cols) * head(2, tile, cols)
            for i in range(2):
                at = slice(i * SEGS, i * SEGS + 1)
                delta_own[i : i + 1, cols] = true_head[i : i + 1] - gated[at, cols]

    def pass_b(tile):
        cols = slice(tile * LANES, (tile + 1) * LANES)
        qtaps = taps_of(0, cols)
        gain = jnp.broadcast_to(skip[0:1, cols], (SEGS, LANES))
        rates, weights, entering = [], [], []
        for n in range(modes):
            entering.append(jnp.where(row >= 1, pltpu.roll(final[n, :, cols], 1, 0), 0.0))
            rates.append(jnp.broadcast_to(jnp.exp(-decay[n : n + 1, cols]), (SEGS, LANES)))
            weights.append(jnp.broadcast_to(weight[n : n + 1, cols], (SEGS, LANES)))

        def respond(j, carry):
            q1, q2, states = carry
            q0 = segments(0, j, tile)
            g = gated[pl.ds(pl.multiple_of(j * SEGS, SEGS), SEGS), cols]
            states = tuple(s * a + g for s, a in zip(states, rates))
            terms = [s * w for s, w in zip(states, weights)] + [gain * g]
            while len(terms) > 1:
                terms = [sum(terms[i : i + 2]) for i in range(0, len(terms), 2)]
            at = pl.ds(j, SEGS, stride=steps)
            base[tile, at] = terms[0]
            qs[tile, at] = short(qtaps, q0, q1, q2)
            return q0, q1, states

        first = (segments(0, -1, tile), segments(0, -2, tile), tuple(entering))
        lax.fori_loop(0, steps, respond, first, unroll=4)

    def corrections(known):
        for t in known:
            for tile in range(tiles):
                half, at = divmod(tile * LANES, part)
                piece = ends[slot(t, half), :, at : at + LANES]
                ends_wide[tile, 8 * t : 8 * t + 8] = piece.astype(f32)
        for tile in range(tiles):
            cols = slice(tile * LANES, (tile + 1) * LANES)
            olds, news = [], []
            for p in (1, 2):
                first, second, before2, before1 = [
                    ends_wide[tile, pl.ds(4 * p - 4 + i, NZ, stride=8)] for i in range(4)
                ]
                line_before = jnp.where(x > 0, ends_wide[tile, 8 * NZ + 4 * p - 2 : 8 * NZ + 4 * p], 0.0)
                before2 = jnp.where(row == 0, line_before[0:1], pltpu.roll(before2, 1, 0))
                before1 = jnp.where(row == 0, line_before[1:2], pltpu.roll(before1, 1, 0))
                now, last1, last2 = [filt[p, i : i + 1, cols] for i in range(3)]
                old0, old1 = now * first, now * second + last1 * first
                olds.append((old0, old1))
                news.append((old0 + last1 * before1 + last2 * before2, old1 + last2 * before1))
            for i in range(2):
                deltas[i, :, cols] = news[0][i] * news[1][i] - olds[0][i] * olds[1][i]

    def own_factors(half):
        rate = decay[:, half * part : (half + 1) * part]
        return jnp.exp(-rate * rows), jnp.exp(-rate * (rows - 1.0)), jnp.exp(-rate * (rows - 2.0))

    def add_line(i, half, carried, block, late0, late1):
        cols = slice(half * part, (half + 1) * part)
        e0, e1 = [deltas[j, i : i + 1, cols] for j in range(2)]
        return carried * block + lines[slot(i, half)] + late0 * e0 + late1 * e1

    def relay_copy(t, half):
        return to_device(
            relayed.at[half], lines.at[slot(RELAY, half)],
            line_send, line_recv.at[1, half], x * NZ + t,
        )

    def relay():
        wait_for(ends_recv.at[0], ends, RELAY * HALVES, RELAY * HALVES)
        for half in range(HALVES):
            wait_for(line_recv.at[0, half], lines, RELAY, RELAY)
        pl.when(x > 0)(tail_line(0).wait_recv)
        corrections([*range(LATE), NZ])
        for half in range(HALVES):
            factors = own_factors(half)
            carried = jnp.zeros((modes, part), f32)
            for i in range(LATE):
                carried = add_line(i, half, carried, *factors)
            relayed[half] = carried
        for t in reversed(later):
            for half in range(HALVES):
                ends_line(t, half).start()
                relay_copy(t, half).start()

    pass_b(0)
    pass_b(1)
    pl.when(z == RELAY)(relay)
    pass_b(2)
    pass_b(3)

    pl.when((z < RELAY) & (x > 0))(tail_line(0).wait_recv)
    def heard(half):
        known = jnp.where(z == RELAY, RELAY, 0)
        return count_of(hears_half(t, half) for t in range(NZ)) - known

    wait_for(ends_recv.at[1], ends, heard(0) + heard(1), NZ + 2)
    corrections(range(NZ + 1))
    def total_copy(k, source, half, shift=0):
        return to_device(
            total.at[half], totals.at[slot(source, half)],
            total_send, total_recv.at[half], me + k * NZ + shift,
        )

    all_factors = [own_factors(half) for half in range(HALVES)]
    hops, into_lines = [], []
    for half in range(HALVES):
        rate = decay[:, half * part : (half + 1) * part]
        hops.append(jnp.exp(-rate * (rows * NZ)))
        into_lines.append(jnp.exp(-rate * (rows * z.astype(f32))))

    def sum_line(half, upto=None):
        factors = all_factors[half]
        carried = jnp.zeros((modes, part), f32)
        for i in range(NZ):
            after = add_line(i, half, carried, *factors)
            if i == RELAY:
                after = jnp.where(early, after, lines[slot(RELAY, half)])
            carried = after if upto is None else jnp.where(upto > i, after, carried)
        return carried

    for half in range(HALVES):
        wait_for(line_recv.at[1, half], lines, heard(half), NZ - 1)

        @pl.when(takes(half) & inner)
        def _(half=half):
            total[half] = sum_line(half)

    pl.when(inner)(lambda: pl.semaphore_wait(ready, 2 * (NX - 1 - x)))
    for half in reversed(range(HALVES)):
        for k in range(1, NX):
            pl.when((x + k < NX) & takes(half))(total_copy(k, x, half, -parity).start)
            pl.when((x + k < NX) & takes(half))(total_copy(k, x, half, 1 - parity).start)

    take_rim()
    d0, d1 = delta_own[0:1], delta_own[1:2]
    inverse = jnp.exp(decay[...])
    rim_state = inverse * (d0 + inverse * d1)
    excess = jnp.sum(weight[...] * inverse, axis=0, keepdims=True) * d1
    for tile in range(tiles):
        cols = slice(tile * LANES, (tile + 1) * LANES)
        base[tile, 0:1] += skip[0:1, cols] * d0[:, cols] - excess[:, cols]
        base[tile, 1:2] += skip[0:1, cols] * d1[:, cols]
        qs[tile, 0:2] = head(0, tile, cols)

    for half in range(HALVES):
        own_sum[half] = sum_line(half, z) + rim_state[:, half * part : (half + 1) * part]

    pl.when(me < last)(rim_copy.wait_send)
    sent = count_of(sends_half(t, half) for t in range(NZ) for half in range(HALVES))
    wait_for(ends_send, ends, sent, NZ + RELAY, send=True)
    wait_for(line_send, lines, sent, NZ + RELAY, send=True)
    wait_for(tail_send, ends, jnp.where(ends_line_here, LATE * HALVES, 0), LATE * HALVES, send=True)

    grow = lax.broadcasted_iota(jnp.int32, (part, part), 0) // modes
    gcol = lax.broadcasted_iota(jnp.int32, (part, part), 1) // size
    for half in reversed(range(HALVES)):
        cols = slice(half * part, (half + 1) * part)
        hop, into_line = hops[half], into_lines[half]
        wait_for(total_recv.at[half], totals, x, NX - 1)
        far = jnp.zeros((modes, part), f32)
        for i in range(NX - 1):
            far = jnp.where(x > i, far * hop + totals[slot(i, half)], far)
        state = own_sum[half] + into_line * far
        blocks = jnp.concatenate([state] * (part // modes), axis=0)
        hi, lo = split(jnp.where(grow == gcol, blocks, 0.0))
        for piece in range(2):
            at = slice(piece * rows // 2, (piece + 1) * rows // 2)
            lh, ll = lead_hi[at, cols], lead_lo[at, cols]
            add = jnp.dot(lh, hi, preferred_element_type=f32)
            add += jnp.dot(lh, lo, preferred_element_type=f32)
            add += jnp.dot(ll, hi, preferred_element_type=f32)
            for t in range(half * part // LANES, (half + 1) * part // LANES):
                more = add[:, t * LANES - half * part : (t + 1) * LANES - half * part]
                out[at, t * LANES : (t + 1) * LANES] = (
                    qs[t, at] * (base[t, at] + more)
                ).astype(jnp.bfloat16)

    wait_for(total_send, totals, 2 * (NX - 1 - x), 2 * (NX - 1), send=True)


def body(query_in, key_in, value_in, residues, decay_rate, short_filter, skip_gain):
    rows, width = query_in.shape
    modes, tiles = residues.shape[0], width // LANES
    pitched = FRONT * SEGS + rows
    half = (modes, width // HALVES)
    f32 = jnp.float32
    vmem = lambda *shape, dtype=f32: pltpu.VMEM(shape, dtype)
    dma = pltpu.SemaphoreType.DMA
    hbm = pl.BlockSpec(memory_space=pltpu.HBM)
    return pl.pallas_call(
        kernel,
        out_shape=jax.ShapeDtypeStruct((rows, width), jnp.bfloat16),
        in_specs=[hbm] * 7,
        out_specs=pl.BlockSpec(memory_space=pltpu.VMEM),
        scratch_shapes=[
            vmem(3, rows, width, dtype=jnp.bfloat16),
            vmem(3, tiles, pitched + FRONT, LANES),
            vmem(*residues.shape),
            vmem(*decay_rate.shape),
            vmem(*short_filter.shape),
            vmem(*skip_gain.shape),
            vmem(modes, width),
            vmem(modes, width),
            vmem(rows, width),
            vmem(modes, SEGS, width),
            vmem(tiles, rows, LANES),
            vmem(tiles, rows, LANES),
            vmem(rows, width, dtype=jnp.bfloat16),
            vmem(rows, width, dtype=jnp.bfloat16),
            vmem(HALVES, *half),
            vmem(NZ * HALVES, *half),
            vmem(HALVES, *half),
            vmem(8, width, dtype=jnp.bfloat16),
            vmem(8, width, dtype=jnp.bfloat16),
            vmem(HALVES, 8, width // HALVES, dtype=jnp.bfloat16),
            vmem((NZ + 1) * HALVES, 8, width // HALVES, dtype=jnp.bfloat16),
            vmem(tiles, NZ * 8 + 8, LANES),
            vmem(2, NZ, width),
            vmem(2, width),
            vmem(HALVES, *half),
            vmem(NX * HALVES, *half),
            vmem(HALVES, *half),
            dma((4,)), dma((HALVES + 1,)),
            dma, dma((2, HALVES)),
            dma, dma((2,)),
            dma, dma,
            dma, dma((HALVES,)),
            dma, dma,
            pltpu.SemaphoreType.REGULAR,
        ],
        compiler_params=pltpu.CompilerParams(
            collective_id=0, has_side_effects=True, vmem_limit_bytes=40 * 2**20
        ),
    )(
        *(
            pltpu.with_memory_space_constraint(a, pltpu.HBM)
            for a in (query_in, key_in, value_in, residues, decay_rate, short_filter, skip_gain)
        )
    )


def solution(mesh):
    placed = (
        P("ctx", "fsdp"),
        P("ctx", "fsdp"),
        P("ctx", "fsdp"),
        P(None, "fsdp"),
        P(None, "fsdp"),
        P(None, None, "fsdp"),
        P(None, "fsdp"),
    )
    return jax.shard_map(
        body, mesh=mesh, in_specs=placed, out_specs=P("ctx", "fsdp"), check_vma=False
    )
```
